256 devices in a mesh: head: 4 (over x), tok: 64 (over z, y, core).
Axes of the slice: x: 4, y: 4, z: 8, core: 2. Of those that a mesh axis runs over, the one named last changes fastest.
Arguments:
- queries: bfloat16 [2, 16384, 5120], P(None, 'tok', 'head'), may hold values from -6 to 6
- key_rows: bfloat16 [16384, 5120], P('tok', 'head'), may hold values from -6 to 6
- value_rows: bfloat16 [16384, 5120], P('tok', 'head'), may hold values from -6 to 6
- step_rates: float32 [20, 16384], P('head', 'tok'), may hold values from 0.05 to 1
- gate_fast: float32 [20, 256, 256], P('head'), may hold values from -0.375 to 0.375
- up_fast: float32 [20, 256, 256], P('head'), may hold values from -0.375 to 0.375
- down_fast: float32 [20, 256, 256], P('head'), may hold values from -0.375 to 0.375
Outputs:
- out_rows: bfloat16 [2, 16384, 5120], P(None, ('tok', 'head'))
The draws below stay inside these ranges and needn't reach their ends.
All inputs are finite; a program needn't handle non-finite values.
Results may differ from the reference program's by a relative error of at most 0.011.
Values may be sent and summed in bfloat16 or wider, within the bound.
No kernel may reach another device: no remote copies, remote signals or barrier semaphores. Data moves between devices by JAX's collectives and lax.ppermute only.
A program may use at most 64 MiB of HBM per device.

```python
import math
import jax
import jax.numpy as jnp
from jax import lax

HD = 256
FH = 256
NS_STEPS = 3
HEADS = 20
BLOCK = 16384


def level_of(own_key, dims, cuts, smallest, largest):
    def one(axis_at, shards_of):
        draws = jax.random.uniform(jax.random.fold_in(jax.random.fold_in(own_key, 6), axis_at), (shards_of,), jnp.float32, smallest / len(cuts), largest / len(cuts))
        return jnp.repeat(jnp.exp(draws), dims[axis_at] // shards_of).reshape((-1,) + (1,) * (len(dims) - axis_at - 1))

    gain = one(*cuts[0])
    for cut in cuts[1:]:
        gain = gain * one(*cut)
    return gain


def noise(own_key, dims, deviation, most, shards=(), dtype=jnp.bfloat16):
    loudness = level_of(own_key, dims, shards, -0.22, 0.18) if shards else 1.0
    array = jax.random.normal(own_key, dims, jnp.float32) * deviation * loudness
    return jnp.minimum(jnp.maximum(array, -most), most).astype(dtype)


def setup_inputs(seed: int = 0) -> dict:
    seeds = jax.random.split(jax.random.key(seed), 8)
    queries = noise(seeds[0], (2, BLOCK, HEADS * HD), 1.0, 6.0, ((1, 64), (2, 4)))
    key_rows = noise(seeds[1], (BLOCK, HEADS * HD), 1.0, 6.0, ((0, 64), (1, 4)))
    value_rows = noise(seeds[2], (BLOCK, HEADS * HD), 1.0, 6.0, ((0, 64), (1, 4)))
    step_rates = jnp.clip(jnp.exp(math.log(1.0) - 2.9957323 * jax.random.uniform(seeds[3], (HEADS, BLOCK), jnp.float32) ** level_of(seeds[3], (HEADS, BLOCK), ((0, 4), (1, 64)), -0.2, 0.2)), 0.05, 1.0)
    gate_fast = noise(seeds[4], (HEADS, HD, FH), HD ** -0.5, 0.375, ((0, 4),), jnp.float32)
    up_fast = noise(seeds[5], (HEADS, HD, FH), HD ** -0.5, 0.375, ((0, 4),), jnp.float32)
    down_fast = noise(seeds[6], (HEADS, FH, HD), FH ** -0.5, 0.375, ((0, 4),), jnp.float32)
    return dict(queries=queries, key_rows=key_rows, value_rows=value_rows, step_rates=step_rates, gate_fast=gate_fast, up_fast=up_fast, down_fast=down_fast)


coef_first = 3.4445
coef_second = -4.775
coef_third = 2.0315

def fast_apply(inputs, gate_mat, up_mat, down_mat):
    gate_pre = jnp.dot(inputs, gate_mat, preferred_element_type=jnp.float32)
    up_pre = jnp.dot(inputs, up_mat, preferred_element_type=jnp.float32)
    hidden = (jax.nn.silu(gate_pre) * up_pre).astype(jnp.bfloat16)
    return jnp.dot(hidden, down_mat, preferred_element_type=jnp.float32).astype(jnp.bfloat16)

def orthogonal(gradient):
    iterate = gradient / (jnp.sqrt(jnp.sum(gradient * gradient)) + 1e-07)
    for sweep in range(NS_STEPS):
        gram = jnp.dot(iterate.T, iterate, precision=lax.Precision.HIGHEST)
        square = jnp.dot(gram, gram, precision=lax.Precision.HIGHEST)
        poly = coef_second * gram + coef_third * square
        iterate = coef_first * iterate + jnp.dot(iterate, poly, precision=lax.Precision.HIGHEST)
    return iterate

def head_layer(pieces):
    first_query, second_query, key_head, value_head, rates, gate_fast, up_fast, down_fast = pieces
    gate_half = gate_fast.astype(jnp.bfloat16)
    up_half = up_fast.astype(jnp.bfloat16)
    down_half = down_fast.astype(jnp.bfloat16)
    first = fast_apply(first_query, gate_half, up_half, down_half)
    gate_pre = jnp.dot(key_head, gate_half, preferred_element_type=jnp.float32)
    up_pre = jnp.dot(key_head, up_half, preferred_element_type=jnp.float32)
    sigmoid_gate = jax.nn.sigmoid(gate_pre)
    hidden = (jax.nn.silu(gate_pre) * up_pre).astype(jnp.bfloat16)
    down_in = (-(rates[:, None] * value_head.astype(jnp.float32))).astype(jnp.bfloat16)
    down_grad = jnp.dot(hidden.T, down_in, preferred_element_type=jnp.float32)
    hidden_grad = jnp.dot(down_in, down_half.T, preferred_element_type=jnp.float32)
    up_in = (hidden_grad * jax.nn.silu(gate_pre)).astype(jnp.bfloat16)
    gate_in = (hidden_grad * up_pre * sigmoid_gate * (1.0 + gate_pre * (1.0 - sigmoid_gate))).astype(jnp.bfloat16)
    gate_grad = jnp.dot(key_head.T, gate_in, preferred_element_type=jnp.float32)
    up_grad = jnp.dot(key_head.T, up_in, preferred_element_type=jnp.float32)
    gate_next = (gate_fast - orthogonal(gate_grad)).astype(jnp.bfloat16)
    up_next = (up_fast - orthogonal(up_grad)).astype(jnp.bfloat16)
    down_next = (down_fast - orthogonal(down_grad)).astype(jnp.bfloat16)
    second = fast_apply(second_query, gate_next, up_next, down_next)
    return (first, second)

def reference(queries, key_rows, value_rows, step_rates, gate_fast, up_fast, down_fast):
    query_heads = queries.reshape(2, BLOCK, HEADS, HD).transpose(2, 0, 1, 3)
    key_heads = key_rows.reshape(BLOCK, HEADS, HD).transpose(1, 0, 2)
    value_heads = value_rows.reshape(BLOCK, HEADS, HD).transpose(1, 0, 2)
    first, second = lax.map(head_layer, (query_heads[:, 0], query_heads[:, 1], key_heads, value_heads, step_rates, gate_fast, up_fast, down_fast))
    joined = jnp.stack((first, second), 0)
    return joined.transpose(0, 2, 1, 3).reshape(2, BLOCK, HEADS * HD)
```

```python
import jax
import jax.numpy as jnp
from jax import lax
from jax.experimental import pallas as pl
from jax.experimental.pallas import tpu as pltpu
from jax.sharding import Mesh, PartitionSpec as P

NS_STEPS = 3
coef_first = 3.4445
coef_second = -4.775
coef_third = 2.0315
F32 = jnp.float32
BF16 = jnp.bfloat16
HD = 256
HALF = 128
HEADS_HERE = 5
MATS = 3 * HEADS_HERE
GROUP = 8
PIECES = 32
VMEM_LIMIT = 48 * 1024 * 1024


def dot_f32(a, b):
    return lax.dot_general(a, b, (((1,), (0,)), ((), ())), preferred_element_type=F32)


def dot_nt(a, b):
    return lax.dot_general(a, b, (((1,), (1,)), ((), ())), preferred_element_type=F32)


def dot_tn(a, b):
    return lax.dot_general(a, b, (((0,), (0,)), ((), ())), preferred_element_type=F32)


def sigmoid(x):
    return 1.0 / (1.0 + jnp.exp(-x))


def apply_fast(rows, gate, up, down):
    zg = dot_f32(rows, gate)
    zu = dot_f32(rows, up)
    hidden = (zg * sigmoid(zg) * zu).astype(BF16)
    return dot_f32(hidden, down).astype(BF16)


def store_rows(out_ref, rows):
    for r in range(out_ref.shape[0]):
        out_ref[r, 0] = rows[r * 64 : (r + 1) * 64, :]


def first_kernel(core_ref, q_ref, k_ref, v_ref, rate_ref, g_ref, u_ref, d_ref, out_ref, keep_ref, send_ref, grad_ref):
    head = pl.program_id(0)
    core = core_ref[0]
    gate = g_ref[0].astype(BF16)
    up = u_ref[0].astype(BF16)
    down = d_ref[0].astype(BF16)
    store_rows(out_ref, apply_fast(q_ref[0], gate, up, down))
    keys = k_ref[...]
    zg = dot_f32(keys, gate)
    zu = dot_f32(keys, up)
    sig = sigmoid(zg)
    silu = zg * sig
    hidden = (silu * zu).astype(BF16)
    rate = rate_ref[pl.ds(head, 1), :]
    rate = jnp.transpose(jnp.broadcast_to(rate, (HALF, rate.shape[1])))
    rate = jnp.concatenate([rate, rate], axis=1)
    dout = (-(rate * v_ref[...].astype(F32))).astype(BF16)
    dh = dot_nt(dout, down)
    dzu = (dh * silu).astype(BF16)
    dzg = (dh * zu * sig * (1.0 + zg * (1.0 - sig))).astype(BF16)
    grad_ref[0] = dot_tn(keys, dzg)
    grad_ref[1] = dot_tn(keys, dzu)
    grad_ref[2] = dot_tn(hidden, dout)
    mine = pl.multiple_of(core * HALF, HALF)
    other = pl.multiple_of((1 - core) * HALF, HALF)
    for mat in range(3):
        for side in range(2):
            cols = slice(side * HALF, (side + 1) * HALF)
            at = slice(side * 16, (side + 1) * 16)
            keep_ref[at, mat] = grad_ref[mat, pl.ds(mine, HALF), cols].reshape(16, 8, HALF)
            send_ref[at, mat] = grad_ref[mat, pl.ds(other, HALF), cols].reshape(16, 8, HALF).astype(BF16)


def split(x):
    high = x.astype(BF16)
    return high, (x - high.astype(F32)).astype(BF16)


def half_matrix(piece):
    piece = piece.astype(F32)
    left = piece[:16].reshape(HALF, HALF)
    right = piece[16:].reshape(HALF, HALF)
    return jnp.concatenate([left, right], axis=1)


def orth_kernel(core_ref, *refs):
    count = (len(refs) - 1) // 2
    out_ref = refs[-1]
    low_core = core_ref[0] == 0
    xs = []
    for i in range(count):
        mine = half_matrix(refs[2 * i][:, 0])
        other = half_matrix(refs[2 * i + 1][:, 0])
        top = jnp.where(low_core, mine, other)
        bottom = jnp.where(low_core, other, mine)
        m = jnp.concatenate([top, bottom], axis=0)
        norm = jnp.sqrt(jnp.sum(m * m, keepdims=True)) + 1e-07
        xs.append(m / norm)
    for sweep in range(NS_STEPS):
        if sweep < NS_STEPS - 1:
            lows = [x.astype(BF16) for x in xs]
            grams = [dot_nt(x, x) for x in lows]
            halves = [a.astype(BF16) for a in grams]
            squares = [dot_f32(a, a) for a in halves]
            polys = [(coef_second * a + coef_third * s).astype(BF16) for a, s in zip(grams, squares)]
            xs = [coef_first * x + dot_f32(p, l) for x, p, l in zip(xs, polys, lows)]
        else:
            parts = [split(x) for x in xs]
            grams = [dot_nt(h, h) + (dot_nt(h, l) + dot_nt(l, h)) for h, l in parts]
            gparts = [split(a) for a in grams]
            squares = [dot_f32(h, h) + (dot_f32(h, l) + dot_f32(l, h)) for h, l in gparts]
            polys = [split(coef_second * a + coef_third * s) for a, s in zip(grams, squares)]
            xs = [
                coef_first * x + (dot_f32(ph, h) + (dot_f32(ph, l) + dot_f32(pw, h)))
                for x, (ph, pw), (h, l) in zip(xs, polys, parts)
            ]
    for i in range(count):
        out_ref[i] = xs[i].astype(BF16)


def second_kernel(core_ref, buf_ref, q_ref, g_ref, u_ref, d_ref, mine_ref, other_ref, out_ref):
    head = pl.program_id(0)
    low_core = core_ref[0] == 0
    nexts = []
    for mat, ref in enumerate((g_ref, u_ref, d_ref)):
        at = head * 3 + mat
        in_low = at < GROUP
        index = jnp.where(in_low, at, at - (GROUP - 1))
        orth = jnp.where(in_low == low_core, mine_ref[index], other_ref[index])
        nexts.append((ref[0] - orth.astype(F32)).astype(BF16))
    store_rows(out_ref, apply_fast(q_ref[0], *nexts))


def local(queries, key_rows, value_rows, step_rates, gate_fast, up_fast, down_fast):
    rows = key_rows.shape[0]
    width = key_rows.shape[1]
    core = lax.axis_index("core").astype(jnp.int32).reshape(1)
    n_head = lax.axis_size("head")
    params = pltpu.CompilerParams(dimension_semantics=("arbitrary",), vmem_limit_bytes=VMEM_LIMIT)
    weight_spec = pl.BlockSpec((1, HD, HD), lambda h, c: (h, 0, 0))
    buf_shape = jax.ShapeDtypeStruct((n_head, 2, rows // n_head, width), BF16)

    def out_spec(block):
        return pl.BlockSpec((n_head, 1, rows // n_head, HD), lambda h, c: (0, block, 0, h))

    piece_spec = pl.BlockSpec((PIECES, 3, 8, HALF), lambda h, c: (0, h, 0, 0))
    buf, keep, send = pl.pallas_call(
        first_kernel,
        grid_spec=pltpu.PrefetchScalarGridSpec(
            num_scalar_prefetch=1,
            grid=(HEADS_HERE,),
            in_specs=[
                pl.BlockSpec((1, rows, HD), lambda h, c: (0, 0, h)),
                pl.BlockSpec((rows, HD), lambda h, c: (0, h)),
                pl.BlockSpec((rows, HD), lambda h, c: (0, h)),
                pl.BlockSpec((HEADS_HERE, rows), lambda h, c: (0, 0)),
                weight_spec,
                weight_spec,
                weight_spec,
            ],
            out_specs=[out_spec(0), piece_spec, piece_spec],
            scratch_shapes=[pltpu.VMEM((3, HD, HD), F32)],
        ),
        out_shape=[
            buf_shape,
            jax.ShapeDtypeStruct((PIECES, MATS, 8, HALF), F32),
            jax.ShapeDtypeStruct((PIECES, MATS, 8, HALF), BF16),
        ],
        compiler_params=params,
        name="first_and_grads",
    )(core, queries, key_rows, value_rows, step_rates, gate_fast, up_fast, down_fast)

    swap = [(0, 1), (1, 0)]
    received = lax.ppermute(send, "core", swap)
    chip_sum = (keep + received.astype(F32)).astype(BF16)
    scattered = lax.all_to_all(chip_sum, ("z", "y"), split_axis=0, concat_axis=0, tiled=True)
    piece = jnp.sum(scattered.astype(F32), axis=0).astype(BF16)
    spread = jnp.broadcast_to(piece[None], (PIECES,) + piece.shape)
    mine = lax.all_to_all(spread, ("z", "y"), split_axis=0, concat_axis=0, tiled=True)
    other = lax.ppermute(mine, "core", swap)

    per_step = 2
    mat_specs = []
    for i in range(per_step):
        spec = pl.BlockSpec((PIECES, 1, 8, HALF), lambda s, c, i=i: (0, c[0] * (GROUP - 1) + s * per_step + i, 0, 0))
        mat_specs += [spec, spec]
    orth_mine = pl.pallas_call(
        orth_kernel,
        grid_spec=pltpu.PrefetchScalarGridSpec(
            num_scalar_prefetch=1,
            grid=(GROUP // per_step,),
            in_specs=mat_specs,
            out_specs=pl.BlockSpec((per_step, HD, HD), lambda s, c: (s, 0, 0)),
        ),
        out_shape=jax.ShapeDtypeStruct((GROUP, HD, HD), BF16),
        compiler_params=params,
        name="orthogonalize",
    )(core, *([mine, other] * per_step))
    orth_other = lax.ppermute(orth_mine, "core", swap)

    group_spec = pl.BlockSpec((GROUP, HD, HD), lambda h, c: (0, 0, 0))
    buf = pl.pallas_call(
        second_kernel,
        grid_spec=pltpu.PrefetchScalarGridSpec(
            num_scalar_prefetch=1,
            grid=(HEADS_HERE,),
            in_specs=[
                pl.BlockSpec(memory_space=pl.ANY),
                pl.BlockSpec((1, rows, HD), lambda h, c: (1, 0, h)),
                weight_spec,
                weight_spec,
                weight_spec,
                group_spec,
                group_spec,
            ],
            out_specs=out_spec(1),
        ),
        out_shape=buf_shape,
        input_output_aliases={1: 0},
        compiler_params=params,
        name="second",
    )(core, buf, queries, gate_fast, up_fast, down_fast, orth_mine, orth_other)

    swapped = lax.all_to_all(buf, "head", split_axis=0, concat_axis=0, tiled=True)
    return swapped.transpose(1, 2, 0, 3).reshape(2, rows // n_head, n_head * width)


def solution(mesh):
    heads = mesh.shape["head"]
    fine = Mesh(mesh.devices.reshape(heads, 8, 4, 2), ("head", "z", "y", "core"))
    tok = ("z", "y", "core")
    placed = (
        P(None, tok, "head"),
        P(tok, "head"),
        P(tok, "head"),
        P("head", tok),
        P("head", None, None),
        P("head", None, None),
        P("head", None, None),
    )
    return jax.shard_map(
        local, mesh=fine, in_specs=placed, out_specs=P(None, tok + ("head",), None), check_vma=False
    )
```

```python
import jax
import jax.numpy as jnp
from jax import lax
from jax.experimental import pallas as pl
from jax.experimental.pallas import tpu as pltpu
from jax.sharding import Mesh, PartitionSpec as P

NS_STEPS = 3
coef_first = 3.4445
coef_second = -4.775
coef_third = 2.0315
F32 = jnp.float32
BF16 = jnp.bfloat16
HD = 256
HALF = 128
HEADS_HERE = 5
MATS = 3 * HEADS_HERE
GROUP = 8
Y = 4
Z = 8
PER_Y = GROUP // Y
ROWS = 64
VMEM_LIMIT = 48 * 1024 * 1024


def dot_f32(a, b):
    return lax.dot_general(a, b, (((1,), (0,)), ((), ())), preferred_element_type=F32)


def dot_nt(a, b):
    return lax.dot_general(a, b, (((1,), (1,)), ((), ())), preferred_element_type=F32)


def dot_tn(a, b):
    return lax.dot_general(a, b, (((0,), (0,)), ((), ())), preferred_element_type=F32)


def sigmoid(x):
    return 0.5 * jnp.tanh(0.5 * x) + 0.5


def apply_fast(rows, gate, up, down):
    zg = dot_f32(rows, gate)
    zu = dot_f32(rows, up)
    hidden = (zg * sigmoid(zg) * zu).astype(BF16)
    return dot_f32(hidden, down).astype(BF16)


def store_rows(out_ref, rows):
    for r in range(out_ref.shape[0]):
        out_ref[r, 0] = rows[r * 64 : (r + 1) * 64, :]


def first_kernel(core_ref, q_ref, k_ref, v_ref, rate_ref, g_ref, u_ref, d_ref, out_ref, keep_ref, send_ref):
    head = pl.program_id(0)
    core = core_ref[0]
    gate = g_ref[0].astype(BF16)
    up = u_ref[0].astype(BF16)
    down = d_ref[0].astype(BF16)
    store_rows(out_ref, apply_fast(q_ref[0], gate, up, down))
    keys = k_ref[...]
    zg = dot_f32(keys, gate)
    zu = dot_f32(keys, up)
    sig = sigmoid(zg)
    silu = zg * sig
    hidden = (silu * zu).astype(BF16)
    rate = rate_ref[pl.ds(head, 1), :]
    rate = jnp.transpose(jnp.broadcast_to(rate, (HALF, rate.shape[1])))
    rate = jnp.concatenate([rate, rate], axis=1)
    dout = (-(rate * v_ref[...].astype(F32))).astype(BF16)
    dh = dot_nt(dout, down)
    dzu = (dh * silu).astype(BF16)
    dzg = (dh * zu * sig * (1.0 + zg * (1.0 - sig))).astype(BF16)
    grads = (dot_tn(keys, dzg), dot_tn(keys, dzu), dot_tn(hidden, dout))
    for mat in range(3):
        grad = grads[mat].astype(BF16)
        at = head * 3 + mat
        for group in range(2):
            slot = at - group * (GROUP - 1)
            inside = (slot >= 0) & (slot < GROUP)
            for ref, wanted in ((keep_ref, core == group), (send_ref, core != group)):

                @pl.when(inside & wanted)
                def _(ref=ref, slot=slot, grad=grad):
                    for z in range(Z):
                        side, block = z // 4, z % 4
                        ref[slot // 2, z, slot % 2] = grad[
                            block * ROWS : (block + 1) * ROWS, side * HALF : (side + 1) * HALF
                        ]


def split(x):
    high = x.astype(BF16)
    return high, (x - high.astype(F32)).astype(BF16)


def orth_kernel(rows_ref, out_ref):
    xs = []
    for i in range(PER_Y):
        sides = [
            jnp.concatenate([rows_ref[side * 4 + block, i].astype(F32) for block in range(4)], axis=0)
            for side in range(2)
        ]
        m = jnp.concatenate(sides, axis=1)
        norm = jnp.sqrt(jnp.sum(m * m, keepdims=True)) + 1e-07
        xs.append(m / norm)
    for sweep in range(NS_STEPS):
        if sweep < NS_STEPS - 1:
            lows = [x.astype(BF16) for x in xs]
            grams = [dot_nt(x, x) for x in lows]
            halves = [a.astype(BF16) for a in grams]
            squares = [dot_f32(a, a) for a in halves]
            polys = [(coef_second * a + coef_third * s).astype(BF16) for a, s in zip(grams, squares)]
            xs = [coef_first * x + dot_f32(p, l) for x, p, l in zip(xs, polys, lows)]
        else:
            parts = [split(x) for x in xs]
            grams = [dot_nt(h, h) + (dot_nt(h, l) + dot_nt(l, h)) for h, l in parts]
            gparts = [split(a) for a in grams]
            squares = [dot_f32(h, h) + (dot_f32(h, l) + dot_f32(l, h)) for h, l in gparts]
            polys = [split(coef_second * a + coef_third * s) for a, s in zip(grams, squares)]
            xs = [
                coef_first * x + (dot_f32(ph, h) + (dot_f32(ph, l) + dot_f32(pw, h)))
                for x, (ph, pw), (h, l) in zip(xs, polys, parts)
            ]
    for i in range(PER_Y):
        for y in range(Y):
            out_ref[y, i] = xs[i].astype(BF16)


def second_kernel(core_ref, buf_ref, q_ref, g_ref, u_ref, d_ref, mine_ref, other_ref, out_ref):
    head = pl.program_id(0)
    low_core = core_ref[0] == 0
    nexts = []
    for mat, ref in enumerate((g_ref, u_ref, d_ref)):
        at = head * 3 + mat
        in_low = at < GROUP
        index = jnp.where(in_low, at, at - (GROUP - 1))
        orth = jnp.where(in_low == low_core, mine_ref[index], other_ref[index])
        nexts.append((ref[0] - orth.astype(F32)).astype(BF16))
    store_rows(out_ref, apply_fast(q_ref[0], *nexts))


def local(queries, key_rows, value_rows, step_rates, gate_fast, up_fast, down_fast):
    rows = key_rows.shape[0]
    width = key_rows.shape[1]
    core = lax.axis_index("core").astype(jnp.int32).reshape(1)
    n_head = lax.axis_size("head")
    params = pltpu.CompilerParams(dimension_semantics=("arbitrary",), vmem_limit_bytes=VMEM_LIMIT)
    weight_spec = pl.BlockSpec((1, HD, HD), lambda h, c: (h, 0, 0))
    buf_shape = jax.ShapeDtypeStruct((n_head, 2, rows // n_head, width), BF16)

    def out_spec(block):
        return pl.BlockSpec((n_head, 1, rows // n_head, HD), lambda h, c: (0, block, 0, h))

    piece_shape = (Y, Z, PER_Y, ROWS, HALF)
    piece_spec = pl.BlockSpec(piece_shape, lambda h, c: (0, 0, 0, 0, 0))
    args = (queries, key_rows, value_rows, step_rates, gate_fast, up_fast, down_fast)
    in_hbm = [pltpu.with_memory_space_constraint(x, pltpu.HBM) for x in args]
    buf, keep, send = pl.pallas_call(
        first_kernel,
        grid_spec=pltpu.PrefetchScalarGridSpec(
            num_scalar_prefetch=1,
            grid=(HEADS_HERE,),
            in_specs=[
                pl.BlockSpec((1, rows, HD), lambda h, c: (0, 0, h)),
                pl.BlockSpec((rows, HD), lambda h, c: (0, h)),
                pl.BlockSpec((rows, HD), lambda h, c: (0, h)),
                pl.BlockSpec((HEADS_HERE, rows), lambda h, c: (0, 0)),
                weight_spec,
                weight_spec,
                weight_spec,
            ],
            out_specs=[out_spec(0), piece_spec, piece_spec],
        ),
        out_shape=[
            buf_shape,
            jax.ShapeDtypeStruct(piece_shape, BF16),
            jax.ShapeDtypeStruct(piece_shape, BF16),
        ],
        compiler_params=params,
        name="first_and_grads",
    )(core, *in_hbm)

    swap = [(0, 1), (1, 0)]
    received = lax.ppermute(send, "core", swap)
    chip_sum = (keep.astype(F32) + received.astype(F32)).astype(BF16)
    by_y = lax.all_to_all(chip_sum, "y", split_axis=0, concat_axis=0, tiled=True)
    y_sum = jnp.sum(by_y.astype(F32), axis=0).astype(BF16)
    by_z = lax.all_to_all(y_sum, "z", split_axis=0, concat_axis=0, tiled=True)
    piece = jnp.sum(by_z.astype(F32), axis=0).astype(BF16)
    spread = jnp.broadcast_to(piece[None], (Z,) + piece.shape)
    whole = lax.all_to_all(spread, "z", split_axis=0, concat_axis=0, tiled=True)

    orth = pl.pallas_call(
        orth_kernel,
        out_shape=jax.ShapeDtypeStruct((Y, PER_Y, HD, HD), BF16),
        compiler_params=pltpu.CompilerParams(vmem_limit_bytes=VMEM_LIMIT),
        name="orthogonalize",
    )(whole)
    orth_mine = lax.all_to_all(orth, "y", split_axis=0, concat_axis=0, tiled=True).reshape(GROUP, HD, HD)
    orth_other = lax.ppermute(orth_mine, "core", swap)

    group_spec = pl.BlockSpec((GROUP, HD, HD), lambda h, c: (0, 0, 0))
    buf = pl.pallas_call(
        second_kernel,
        grid_spec=pltpu.PrefetchScalarGridSpec(
            num_scalar_prefetch=1,
            grid=(HEADS_HERE,),
            in_specs=[
                pl.BlockSpec(memory_space=pl.ANY),
                pl.BlockSpec((1, rows, HD), lambda h, c: (1, 0, h)),
                weight_spec,
                weight_spec,
                weight_spec,
                group_spec,
                group_spec,
            ],
            out_specs=out_spec(1),
        ),
        out_shape=buf_shape,
        input_output_aliases={1: 0},
        compiler_params=params,
        name="second",
    )(core, buf, queries, gate_fast, up_fast, down_fast, orth_mine, orth_other)

    swapped = lax.all_to_all(buf, "head", split_axis=0, concat_axis=0, tiled=True)
    return swapped.transpose(1, 2, 0, 3).reshape(2, rows // n_head, n_head * width)


def solution(mesh):
    heads = mesh.shape["head"]
    fine = Mesh(mesh.devices.reshape(heads, 8, 4, 2), ("head", "z", "y", "core"))
    tok = ("z", "y", "core")
    placed = (
        P(None, tok, "head"),
        P(tok, "head"),
        P(tok, "head"),
        P("head", tok),
        P("head", None, None),
        P("head", None, None),
        P("head", None, None),
    )
    return jax.shard_map(
        local, mesh=fine, in_specs=placed, out_specs=P(None, tok + ("head",), None), check_vma=False
    )
```

```python
import jax
import jax.numpy as jnp
from jax import lax
from jax.experimental import pallas as pl
from jax.experimental.pallas import tpu as pltpu
from jax.sharding import Mesh, PartitionSpec as P

NS_STEPS = 3
coef_first = 3.4445
coef_second = -4.775
coef_third = 2.0315
F32 = jnp.float32
BF16 = jnp.bfloat16
HD = 256
HALF = 128
HEADS_HERE = 5
MATS = 3 * HEADS_HERE
GROUP = 8
Y = 4
Z = 8
PER_Y = GROUP // Y
OWN_HEADS = 2
ROWS = 64
VMEM_LIMIT = 48 * 1024 * 1024


def dot_f32(a, b):
    return lax.dot_general(a, b, (((1,), (0,)), ((), ())), preferred_element_type=F32)


def dot_nt(a, b):
    return lax.dot_general(a, b, (((1,), (1,)), ((), ())), preferred_element_type=F32)


def dot_tn(a, b):
    return lax.dot_general(a, b, (((0,), (0,)), ((), ())), preferred_element_type=F32)


def sigmoid(x):
    return 0.5 * jnp.tanh(0.5 * x) + 0.5


def apply_fast(rows, gate, up, down):
    zg = dot_f32(rows, gate)
    zu = dot_f32(rows, up)
    hidden = (zg * sigmoid(zg) * zu).astype(BF16)
    return dot_f32(hidden, down).astype(BF16)


def first_kernel(q_ref, g_ref, u_ref, d_ref, out_ref):
    weights = [ref[0].astype(BF16) for ref in (g_ref, u_ref, d_ref)]
    out_ref[...] = apply_fast(q_ref[0], *weights)


def grad_kernel(core_ref, k_ref, v_ref, rate_ref, g_ref, u_ref, d_ref, keep_ref, send_ref):
    head = pl.program_id(0)
    core = core_ref[0]
    gate = g_ref[0].astype(BF16)
    up = u_ref[0].astype(BF16)
    down = d_ref[0].astype(BF16)
    keys = k_ref[...]
    zg = dot_f32(keys, gate)
    zu = dot_f32(keys, up)
    sig = sigmoid(zg)
    silu = zg * sig
    hidden = (silu * zu).astype(BF16)
    rate = rate_ref[pl.ds(head, 1), :]
    rate = jnp.transpose(jnp.broadcast_to(rate, (HALF, rate.shape[1])))
    rate = jnp.concatenate([rate, rate], axis=1)
    dout = (-(rate * v_ref[...].astype(F32))).astype(BF16)
    dh = dot_nt(dout, down)
    dzu = (dh * silu).astype(BF16)
    dzg = (dh * zu * sig * (1.0 + zg * (1.0 - sig))).astype(BF16)
    pair = dot_tn(keys, jnp.concatenate([dzg, dzu], axis=1)).astype(BF16)
    grads = (pair[:, :HD], pair[:, HD:], dot_tn(hidden, dout).astype(BF16))
    for mat in range(3):
        grad = grads[mat]
        at = head * 3 + mat
        for group in range(2):
            slot = at - group * (GROUP - 1)
            inside = (slot >= 0) & (slot < GROUP)
            for ref, wanted in ((keep_ref, core == group), (send_ref, core != group)):

                @pl.when(inside & wanted)
                def _(ref=ref, slot=slot, grad=grad):
                    for z in range(Z):
                        side, block = z // 4, z % 4
                        ref[slot // 2, z, slot % 2] = grad[
                            block * ROWS : (block + 1) * ROWS, side * HALF : (side + 1) * HALF
                        ]


def split(x):
    high = x.astype(BF16)
    return high, (x - high.astype(F32)).astype(BF16)


def orth_kernel(rows_ref, out_ref):
    xs = []
    for i in range(PER_Y):
        sides = [
            jnp.concatenate([rows_ref[side * 4 + block, i].astype(F32) for block in range(4)], axis=0)
            for side in range(2)
        ]
        m = jnp.concatenate(sides, axis=1)
        norm = jnp.sqrt(jnp.sum(m * m, keepdims=True)) + 1e-07
        xs.append(m / norm)
    for sweep in range(NS_STEPS):
        if sweep < NS_STEPS - 1:
            lows = [x.astype(BF16) for x in xs]
            grams = [dot_nt(x, x) for x in lows]
            halves = [a.astype(BF16) for a in grams]
            squares = [dot_f32(a, a) for a in halves]
            polys = [(coef_second * a + coef_third * s).astype(BF16) for a, s in zip(grams, squares)]
            xs = [coef_first * x + dot_f32(p, l) for x, p, l in zip(xs, polys, lows)]
        else:
            parts = [split(x) for x in xs]
            grams = [dot_nt(h, h) + (dot_nt(h, l) + dot_nt(l, h)) for h, l in parts]
            gparts = [split(a) for a in grams]
            squares = [dot_f32(h, h) + (dot_f32(h, l) + dot_f32(l, h)) for h, l in gparts]
            polys = [split(coef_second * a + coef_third * s) for a, s in zip(grams, squares)]
            xs = [
                coef_first * x + (dot_f32(ph, h) + (dot_f32(ph, l) + dot_f32(pw, h)))
                for x, (ph, pw), (h, l) in zip(xs, polys, parts)
            ]
    for i in range(PER_Y):
        for y in range(Y):
            out_ref[y, i] = xs[i].astype(BF16)


def next_weight(fast, orth):
    return (fast - orth.astype(F32)).astype(BF16)


def own_second_kernel(core_ref, heads_ref, q_ref, g_ref, u_ref, d_ref, mine_ref, out_ref):
    head = heads_ref[pl.program_id(0)]
    base = head * 3 - core_ref[0] * (GROUP - 1)
    nexts = [next_weight(ref[0], mine_ref[base + mat]) for mat, ref in enumerate((g_ref, u_ref, d_ref))]
    out_ref[...] = apply_fast(q_ref[0], *nexts)


def rest_second_kernel(core_ref, heads_ref, buf_ref, q_ref, g_ref, u_ref, d_ref, mine_ref, other_ref, out_ref):
    head = heads_ref[OWN_HEADS + pl.program_id(0)]
    low_core = core_ref[0] == 0
    nexts = []
    for mat, ref in enumerate((g_ref, u_ref, d_ref)):
        at = head * 3 + mat
        in_low = at < GROUP
        index = jnp.where(in_low, at, at - (GROUP - 1))
        orth = jnp.where(in_low == low_core, mine_ref[index], other_ref[index])
        nexts.append(next_weight(ref[0], orth))
    out_ref[...] = apply_fast(q_ref[0], *nexts)


def join_kernel(place_ref, first_ref, second_ref, out_ref):
    out_ref[0] = first_ref[0]
    out_ref[1] = second_ref[0]


def local(queries, key_rows, value_rows, step_rates, gate_fast, up_fast, down_fast):
    rows = key_rows.shape[0]
    width = key_rows.shape[1]
    core = lax.axis_index("core").astype(jnp.int32).reshape(1)
    n_head = lax.axis_size("head")
    part = rows // n_head
    params = pltpu.CompilerParams(dimension_semantics=("arbitrary",), vmem_limit_bytes=VMEM_LIMIT)
    weight_spec = pl.BlockSpec((1, HD, HD), lambda h, *_: (h, 0, 0))
    rows_spec = pl.BlockSpec((rows, HD), lambda h, *_: (0, h))
    rows_shape = jax.ShapeDtypeStruct((rows, width), BF16)

    piece_shape = (Y, Z, PER_Y, ROWS, HALF)
    piece_spec = pl.BlockSpec(piece_shape, lambda h, c: (0, 0, 0, 0, 0))
    args = (queries, key_rows, value_rows, step_rates, gate_fast, up_fast, down_fast)
    q_hbm, k_hbm, v_hbm, rate_hbm, g_hbm, u_hbm, d_hbm = [
        pltpu.with_memory_space_constraint(x, pltpu.HBM) for x in args
    ]
    keep, send = pl.pallas_call(
        grad_kernel,
        grid_spec=pltpu.PrefetchScalarGridSpec(
            num_scalar_prefetch=1,
            grid=(HEADS_HERE,),
            in_specs=[
                rows_spec,
                rows_spec,
                pl.BlockSpec((HEADS_HERE, rows), lambda h, c: (0, 0)),
                weight_spec,
                weight_spec,
                weight_spec,
            ],
            out_specs=[piece_spec, piece_spec],
        ),
        out_shape=[jax.ShapeDtypeStruct(piece_shape, BF16), jax.ShapeDtypeStruct(piece_shape, BF16)],
        compiler_params=params,
        name="grads",
    )(core, k_hbm, v_hbm, rate_hbm, g_hbm, u_hbm, d_hbm)

    swap = [(0, 1), (1, 0)]
    received = lax.ppermute(send, "core", swap)
    first = pl.pallas_call(
        first_kernel,
        grid=(HEADS_HERE,),
        in_specs=[pl.BlockSpec((1, rows, HD), lambda h: (0, 0, h)), weight_spec, weight_spec, weight_spec],
        out_specs=rows_spec,
        out_shape=rows_shape,
        compiler_params=params,
        name="first",
    )(q_hbm, g_hbm, u_hbm, d_hbm)
    first_all = lax.all_gather(first, "head", axis=0)

    chip_sum = (keep.astype(F32) + received.astype(F32)).astype(BF16)
    by_y = lax.all_to_all(chip_sum, "y", split_axis=0, concat_axis=0, tiled=True)
    y_sum = jnp.sum(by_y.astype(F32), axis=0).astype(BF16)
    by_z = lax.all_to_all(y_sum, "z", split_axis=0, concat_axis=0, tiled=True)
    piece = jnp.sum(by_z.astype(F32), axis=0).astype(BF16)
    spread = jnp.broadcast_to(piece[None], (Z,) + piece.shape)
    whole = lax.all_to_all(spread, "z", split_axis=0, concat_axis=0, tiled=True)

    orth = pl.pallas_call(
        orth_kernel,
        out_shape=jax.ShapeDtypeStruct((Y, PER_Y, HD, HD), BF16),
        compiler_params=pltpu.CompilerParams(vmem_limit_bytes=VMEM_LIMIT),
        name="orthogonalize",
    )(whole)
    orth_mine = lax.all_to_all(orth, "y", split_axis=0, concat_axis=0, tiled=True).reshape(GROUP, HD, HD)
    orth_other = lax.ppermute(orth_mine, "core", swap)

    def second_specs(start):
        def at(s, heads):
            return heads[start + s]

        query = pl.BlockSpec((1, rows, HD), lambda s, c, heads: (1, 0, at(s, heads)))
        weight = pl.BlockSpec((1, HD, HD), lambda s, c, heads: (at(s, heads), 0, 0))
        out = pl.BlockSpec((rows, HD), lambda s, c, heads: (0, at(s, heads)))
        return [query, weight, weight, weight], out

    heads = (jnp.arange(HEADS_HERE, dtype=jnp.int32) + core * (HEADS_HERE - OWN_HEADS)) % HEADS_HERE
    group_spec = pl.BlockSpec((GROUP, HD, HD), lambda s, c, heads: (0, 0, 0))
    specs, out_spec = second_specs(0)
    second = pl.pallas_call(
        own_second_kernel,
        grid_spec=pltpu.PrefetchScalarGridSpec(
            num_scalar_prefetch=2, grid=(OWN_HEADS,), in_specs=specs + [group_spec], out_specs=out_spec
        ),
        out_shape=rows_shape,
        compiler_params=params,
        name="second_own",
    )(core, heads, queries, gate_fast, up_fast, down_fast, orth_mine)
    specs, out_spec = second_specs(OWN_HEADS)
    second = pl.pallas_call(
        rest_second_kernel,
        grid_spec=pltpu.PrefetchScalarGridSpec(
            num_scalar_prefetch=2,
            grid=(HEADS_HERE - OWN_HEADS,),
            in_specs=[pl.BlockSpec(memory_space=pl.ANY)] + specs + [group_spec, group_spec],
            out_specs=out_spec,
        ),
        out_shape=rows_shape,
        input_output_aliases={2: 0},
        compiler_params=params,
        name="second_rest",
    )(core, heads, second, queries, gate_fast, up_fast, down_fast, orth_mine, orth_other)

    swapped = lax.all_to_all(second.reshape(n_head, part, width), "head", split_axis=0, concat_axis=0, tiled=True)
    place = lax.axis_index("head").astype(jnp.int32).reshape(1)
    return pl.pallas_call(
        join_kernel,
        grid_spec=pltpu.PrefetchScalarGridSpec(
            num_scalar_prefetch=1,
            grid=(n_head,),
            in_specs=[
                pl.BlockSpec((1, part, width), lambda s, p: (s, p[0], 0)),
                pl.BlockSpec((1, part, width), lambda s, p: (s, 0, 0)),
            ],
            out_specs=pl.BlockSpec((2, part, width), lambda s, p: (0, 0, s)),
        ),
        out_shape=jax.ShapeDtypeStruct((2, part, n_head * width), BF16),
        compiler_params=params,
        name="join",
    )(place, pltpu.with_memory_space_constraint(first_all, pltpu.HBM), swapped)


def solution(mesh):
    heads = mesh.shape["head"]
    fine = Mesh(mesh.devices.reshape(heads, 8, 4, 2), ("head", "z", "y", "core"))
    tok = ("z", "y", "core")
    placed = (
        P(None, tok, "head"),
        P(tok, "head"),
        P(tok, "head"),
        P("head", tok),
        P("head", None, None),
        P("head", None, None),
        P("head", None, None),
    )
    return jax.shard_map(
        local, mesh=fine, in_specs=placed, out_specs=P(None, tok + ("head",), None), check_vma=False
    )
```

```python
import jax
import jax.numpy as jnp
from jax import lax
from jax.experimental import pallas as pl
from jax.experimental.pallas import tpu as pltpu
from jax.sharding import Mesh, PartitionSpec as P

NS_STEPS = 3
coef_first = 3.4445
coef_second = -4.775
coef_third = 2.0315
F32 = jnp.float32
BF16 = jnp.bfloat16
HD = 256
HALF = 128
HEADS_HERE = 5
MATS = 3 * HEADS_HERE
GROUP = 8
Y = 4
Z = 8
PER_Y = GROUP // Y
ROWS = 64
VMEM_LIMIT = 48 * 1024 * 1024


def dot_f32(a, b):
    return lax.dot_general(a, b, (((1,), (0,)), ((), ())), preferred_element_type=F32)


def dot_nt(a, b):
    return lax.dot_general(a, b, (((1,), (1,)), ((), ())), preferred_element_type=F32)


def dot_tn(a, b):
    return lax.dot_general(a, b, (((0,), (0,)), ((), ())), preferred_element_type=F32)


def sigmoid(x):
    return 0.5 * jnp.tanh(0.5 * x) + 0.5


def apply_fast(rows, gate, up, down):
    zg = dot_f32(rows, gate)
    zu = dot_f32(rows, up)
    hidden = (zg * sigmoid(zg) * zu).astype(BF16)
    return dot_f32(hidden, down).astype(BF16)


def first_kernel(place_ref, q_ref, g_ref, u_ref, d_ref, *refs):
    out_refs, rows_ref = refs[:-1], refs[-1]
    weights = [ref[0].astype(BF16) for ref in (g_ref, u_ref, d_ref)]
    rows_ref[...] = apply_fast(q_ref[0], *weights)
    count = len(out_refs)
    part = rows_ref.shape[0] // count
    for hop, out_ref in enumerate(out_refs):
        to = lax.rem(place_ref[0] + hop, count)
        out_ref[...] = rows_ref[pl.ds(pl.multiple_of(to * part, part), part), :]


def grad_kernel(core_ref, k_ref, v_ref, rate_ref, g_ref, u_ref, d_ref, keep_ref, send_ref):
    head = pl.program_id(0)
    core = core_ref[0]
    gate = g_ref[0].astype(BF16)
    up = u_ref[0].astype(BF16)
    down = d_ref[0].astype(BF16)
    keys = k_ref[...]
    zg = dot_f32(keys, gate)
    zu = dot_f32(keys, up)
    sig = sigmoid(zg)
    silu = zg * sig
    hidden = (silu * zu).astype(BF16)
    rate = rate_ref[pl.ds(head, 1), :]
    rate = jnp.transpose(jnp.broadcast_to(rate, (HALF, rate.shape[1])))
    rate = jnp.concatenate([rate, rate], axis=1)
    dout = (-(rate * v_ref[...].astype(F32))).astype(BF16)
    dh = dot_nt(dout, down)
    dzu = (dh * silu).astype(BF16)
    dzg = (dh * zu * sig * (1.0 + zg * (1.0 - sig))).astype(BF16)
    pair = dot_tn(keys, jnp.concatenate([dzg, dzu], axis=1)).astype(BF16)
    grads = (pair[:, :HD], pair[:, HD:], dot_tn(hidden, dout).astype(BF16))
    for mat in range(3):
        grad = grads[mat]
        at = head * 3 + mat
        for group in range(2):
            slot = at - group * (GROUP - 1)
            inside = (slot >= 0) & (slot < GROUP)
            for ref, wanted in ((keep_ref, core == group), (send_ref, core != group)):

                @pl.when(inside & wanted)
                def _(ref=ref, slot=slot, grad=grad):
                    for z in range(Z):
                        side, block = z // 4, z % 4
                        ref[slot // 2, z, slot % 2] = grad[
                            block * ROWS : (block + 1) * ROWS, side * HALF : (side + 1) * HALF
                        ]


def split(x):
    high = x.astype(BF16)
    return high, (x - high.astype(F32)).astype(BF16)


def orth_kernel(rows_ref, out_ref):
    xs = []
    for i in range(PER_Y):
        sides = [
            jnp.concatenate([rows_ref[side * 4 + block, i].astype(F32) for block in range(4)], axis=0)
            for side in range(2)
        ]
        m = jnp.concatenate(sides, axis=1)
        norm = jnp.sqrt(jnp.sum(m * m, keepdims=True)) + 1e-07
        xs.append(m / norm)
    for sweep in range(NS_STEPS):
        if sweep < NS_STEPS - 1:
            lows = [x.astype(BF16) for x in xs]
            grams = [dot_nt(x, x) for x in lows]
            halves = [a.astype(BF16) for a in grams]
            squares = [dot_f32(a, a) for a in halves]
            polys = [(coef_second * a + coef_third * s).astype(BF16) for a, s in zip(grams, squares)]
            xs = [coef_first * x + dot_f32(p, l) for x, p, l in zip(xs, polys, lows)]
        else:
            parts = [split(x) for x in xs]
            grams = [dot_nt(h, h) + (dot_nt(h, l) + dot_nt(l, h)) for h, l in parts]
            gparts = [split(a) for a in grams]
            squares = [dot_f32(h, h) + (dot_f32(h, l) + dot_f32(l, h)) for h, l in gparts]
            polys = [split(coef_second * a + coef_third * s) for a, s in zip(grams, squares)]
            xs = [
                coef_first * x + (dot_f32(ph, h) + (dot_f32(ph, l) + dot_f32(pw, h)))
                for x, (ph, pw), (h, l) in zip(xs, polys, parts)
            ]
    for i in range(PER_Y):
        for y in range(Y):
            out_ref[y, i] = xs[i].astype(BF16)


def next_weight(fast, orth):
    return (fast - orth.astype(F32)).astype(BF16)


def second_kernel(core_ref, q_ref, g_ref, u_ref, d_ref, mine_ref, other_ref, out_ref):
    head = pl.program_id(0)
    low_core = core_ref[0] == 0
    nexts = []
    for mat, ref in enumerate((g_ref, u_ref, d_ref)):
        at = head * 3 + mat
        in_low = at < GROUP
        index = jnp.where(in_low, at, at - (GROUP - 1))
        orth = jnp.where(in_low == low_core, mine_ref[index], other_ref[index])
        nexts.append(next_weight(ref[0], orth))
    out_ref[...] = apply_fast(q_ref[0], *nexts)


def lay_first_kernel(place_ref, *refs):
    hop = pl.program_id(0)
    for i, ref in enumerate(refs[:-1]):

        @pl.when(hop == i)
        def _(ref=ref):
            refs[-1][0] = ref[...]


def lay_second_kernel(buf_ref, rows_ref, out_ref):
    out_ref[...] = rows_ref[...]


def local(queries, key_rows, value_rows, step_rates, gate_fast, up_fast, down_fast):
    rows = key_rows.shape[0]
    width = key_rows.shape[1]
    core = lax.axis_index("core").astype(jnp.int32).reshape(1)
    n_head = lax.axis_size("head")
    part = rows // n_head
    params = pltpu.CompilerParams(dimension_semantics=("arbitrary",), vmem_limit_bytes=VMEM_LIMIT)
    weight_spec = pl.BlockSpec((1, HD, HD), lambda h, *_: (h, 0, 0))
    rows_spec = pl.BlockSpec((rows, HD), lambda h, *_: (0, h))
    rows_shape = jax.ShapeDtypeStruct((rows, width), BF16)

    piece_shape = (Y, Z, PER_Y, ROWS, HALF)
    piece_spec = pl.BlockSpec(piece_shape, lambda h, c: (0, 0, 0, 0, 0))
    args = (queries, key_rows, value_rows, step_rates, gate_fast, up_fast, down_fast)
    q_hbm, k_hbm, v_hbm, rate_hbm, g_hbm, u_hbm, d_hbm = [
        pltpu.with_memory_space_constraint(x, pltpu.HBM) for x in args
    ]
    keep, send = pl.pallas_call(
        grad_kernel,
        grid_spec=pltpu.PrefetchScalarGridSpec(
            num_scalar_prefetch=1,
            grid=(HEADS_HERE,),
            in_specs=[
                rows_spec,
                rows_spec,
                pl.BlockSpec((HEADS_HERE, rows), lambda h, c: (0, 0)),
                weight_spec,
                weight_spec,
                weight_spec,
            ],
            out_specs=[piece_spec, piece_spec],
        ),
        out_shape=[jax.ShapeDtypeStruct(piece_shape, BF16), jax.ShapeDtypeStruct(piece_shape, BF16)],
        compiler_params=params,
        name="grads",
    )(core, k_hbm, v_hbm, rate_hbm, g_hbm, u_hbm, d_hbm)

    swap = [(0, 1), (1, 0)]
    received = lax.ppermute(send, "core", swap)
    place = lax.axis_index("head").astype(jnp.int32).reshape(1)
    part_spec = pl.BlockSpec((part, HD), lambda h, p: (0, h))
    firsts = pl.pallas_call(
        first_kernel,
        grid_spec=pltpu.PrefetchScalarGridSpec(
            num_scalar_prefetch=1,
            grid=(HEADS_HERE,),
            in_specs=[pl.BlockSpec((1, rows, HD), lambda h, p: (0, 0, h)), weight_spec, weight_spec, weight_spec],
            out_specs=[part_spec] * n_head,
            scratch_shapes=[pltpu.VMEM((rows, HD), BF16)],
        ),
        out_shape=[jax.ShapeDtypeStruct((part, width), BF16)] * n_head,
        compiler_params=params,
        name="first",
    )(place, q_hbm, g_hbm, u_hbm, d_hbm)
    firsts = [firsts[0]] + [
        lax.ppermute(firsts[hop], "head", [(i, (i + hop) % n_head) for i in range(n_head)])
        for hop in range(1, n_head)
    ]

    chip_sum = (keep.astype(F32) + received.astype(F32)).astype(BF16)
    by_y = lax.all_to_all(chip_sum, "y", split_axis=0, concat_axis=0, tiled=True)
    by_y, *firsts = lax.optimization_barrier((by_y, *firsts))
    y_sum = jnp.sum(by_y.astype(F32), axis=0).astype(BF16)
    by_z = lax.all_to_all(y_sum, "z", split_axis=0, concat_axis=0, tiled=True)
    piece = jnp.sum(by_z.astype(F32), axis=0).astype(BF16)
    spread = jnp.broadcast_to(piece[None], (Z,) + piece.shape)
    whole = lax.all_to_all(spread, "z", split_axis=0, concat_axis=0, tiled=True)

    orth = pl.pallas_call(
        orth_kernel,
        out_shape=jax.ShapeDtypeStruct((Y, PER_Y, HD, HD), BF16),
        compiler_params=pltpu.CompilerParams(vmem_limit_bytes=VMEM_LIMIT),
        name="orthogonalize",
    )(whole)
    orth_mine = lax.all_to_all(orth, "y", split_axis=0, concat_axis=0, tiled=True).reshape(GROUP, HD, HD)
    orth_other = lax.ppermute(orth_mine, "core", swap)

    group_spec = pl.BlockSpec((GROUP, HD, HD), lambda h, c: (0, 0, 0))
    second = pl.pallas_call(
        second_kernel,
        grid_spec=pltpu.PrefetchScalarGridSpec(
            num_scalar_prefetch=1,
            grid=(HEADS_HERE,),
            in_specs=[pl.BlockSpec((1, rows, HD), lambda h, c: (1, 0, h))] + [weight_spec] * 3 + [group_spec] * 2,
            out_specs=rows_spec,
        ),
        out_shape=rows_shape,
        compiler_params=params,
        name="second",
    )(core, queries, gate_fast, up_fast, down_fast, orth_mine, orth_other)

    swapped = lax.all_to_all(second.reshape(n_head, part, width), "head", split_axis=0, concat_axis=0, tiled=True)
    out_shape = jax.ShapeDtypeStruct((2, part, n_head * width), BF16)
    out = pl.pallas_call(
        lay_first_kernel,
        grid_spec=pltpu.PrefetchScalarGridSpec(
            num_scalar_prefetch=1,
            grid=(n_head,),
            in_specs=[pl.BlockSpec((part, width), lambda s, p: (0, 0))] * n_head,
            out_specs=pl.BlockSpec((1, part, width), lambda s, p: (0, 0, lax.rem(p[0] + n_head - s, n_head))),
        ),
        out_shape=out_shape,
        compiler_params=params,
        name="lay_first",
    )(place, *firsts)
    return pl.pallas_call(
        lay_second_kernel,
        grid=(n_head,),
        in_specs=[
            pl.BlockSpec(memory_space=pl.ANY),
            pl.BlockSpec((1, part, width), lambda s: (s, 0, 0)),
        ],
        out_specs=pl.BlockSpec((1, part, width), lambda s: (1, 0, s)),
        out_shape=out_shape,
        input_output_aliases={0: 0},
        compiler_params=params,
        name="lay_second",
    )(out, swapped)


def solution(mesh):
    heads = mesh.shape["head"]
    fine = Mesh(mesh.devices.reshape(heads, 8, 4, 2), ("head", "z", "y", "core"))
    tok = ("z", "y", "core")
    placed = (
        P(None, tok, "head"),
        P(tok, "head"),
        P(tok, "head"),
        P("head", tok),
        P("head", None, None),
        P("head", None, None),
        P("head", None, None),
    )
    return jax.shard_map(
        local, mesh=fine, in_specs=placed, out_specs=P(None, tok + ("head",), None), check_vma=False
    )
```

```python
import jax
import jax.numpy as jnp
from jax import lax
from jax.experimental import pallas as pl
from jax.experimental.pallas import tpu as pltpu
from jax.sharding import Mesh, PartitionSpec as P

NS_STEPS = 3
coef_first = 3.4445
coef_second = -4.775
coef_third = 2.0315
F32 = jnp.float32
BF16 = jnp.bfloat16
HD = 256
HALF = 128
HEADS_HERE = 5
MATS = 3 * HEADS_HERE
GROUP = 8
VMEM_LIMIT = 48 * 1024 * 1024


def dot_f32(a, b):
    return lax.dot_general(a, b, (((1,), (0,)), ((), ())), preferred_element_type=F32)


def dot_nt(a, b):
    return lax.dot_general(a, b, (((1,), (1,)), ((), ())), preferred_element_type=F32)


def dot_tn(a, b):
    return lax.dot_general(a, b, (((0,), (0,)), ((), ())), preferred_element_type=F32)


def sigmoid(x):
    return 0.5 * jnp.tanh(0.5 * x) + 0.5


def apply_fast(rows, gate, up, down):
    zg = dot_f32(rows, gate)
    zu = dot_f32(rows, up)
    hidden = (zg * sigmoid(zg) * zu).astype(BF16)
    return dot_f32(hidden, down).astype(BF16)


def first_kernel(place_ref, q_ref, g_ref, u_ref, d_ref, *refs):
    out_refs, rows_ref = refs[:-1], refs[-1]
    weights = [ref[0].astype(BF16) for ref in (g_ref, u_ref, d_ref)]
    rows_ref[...] = apply_fast(q_ref[0], *weights)
    count = len(out_refs)
    part = rows_ref.shape[0] // count
    for hop, out_ref in enumerate(out_refs):
        to = lax.rem(place_ref[0] + hop, count)
        out_ref[...] = rows_ref[pl.ds(pl.multiple_of(to * part, part), part), :]


def grad_kernel(core_ref, k_ref, v_ref, rate_ref, g_ref, u_ref, d_ref, keep_ref, send_ref):
    head = pl.program_id(0)
    core = core_ref[0]
    gate = g_ref[0].astype(BF16)
    up = u_ref[0].astype(BF16)
    down = d_ref[0].astype(BF16)
    keys = k_ref[...]
    zg = dot_f32(keys, gate)
    zu = dot_f32(keys, up)
    sig = sigmoid(zg)
    silu = zg * sig
    hidden = (silu * zu).astype(BF16)
    rate = rate_ref[pl.ds(head, 1), :]
    rate = jnp.transpose(jnp.broadcast_to(rate, (HALF, rate.shape[1])))
    rate = jnp.concatenate([rate, rate], axis=1)
    dout = (-(rate * v_ref[...].astype(F32))).astype(BF16)
    dh = dot_nt(dout, down)
    dzu = (dh * silu).astype(BF16)
    dzg = (dh * zu * sig * (1.0 + zg * (1.0 - sig))).astype(BF16)
    pair = dot_tn(keys, jnp.concatenate([dzg, dzu], axis=1)).astype(BF16)
    grads = (pair[:, :HD], pair[:, HD:], dot_tn(hidden, dout).astype(BF16))
    for mat in range(3):
        grad = grads[mat]
        at = head * 3 + mat
        for group in range(2):
            slot = at - group * (GROUP - 1)
            inside = (slot >= 0) & (slot < GROUP)
            for ref, wanted in ((keep_ref, core == group), (send_ref, core != group)):

                @pl.when(inside & wanted)
                def _(ref=ref, slot=slot, grad=grad):
                    ref[slot] = grad


def split(x):
    high = x.astype(BF16)
    return high, (x - high.astype(F32)).astype(BF16)


def orth_kernel(*refs):
    out_ref = refs[-1]
    m = refs[0][...].astype(F32)
    for ref in refs[1:-1]:
        m = m + ref[...].astype(F32)
    x = m / (jnp.sqrt(jnp.sum(m * m, keepdims=True)) + 1e-07)
    for sweep in range(NS_STEPS):
        if sweep < NS_STEPS - 1:
            low = x.astype(BF16)
            gram = dot_nt(low, low)
            half = gram.astype(BF16)
            poly = (coef_second * gram + coef_third * dot_f32(half, half)).astype(BF16)
            x = coef_first * x + dot_f32(poly, low)
        else:
            h, l = split(x)
            gram = dot_nt(h, h) + (dot_nt(h, l) + dot_nt(l, h))
            gh, gl = split(gram)
            square = dot_f32(gh, gh) + (dot_f32(gh, gl) + dot_f32(gl, gh))
            ph, pw = split(coef_second * gram + coef_third * square)
            x = coef_first * x + (dot_f32(ph, h) + (dot_f32(ph, l) + dot_f32(pw, h)))
    orth = x.astype(BF16)
    for i in range(out_ref.shape[0]):
        out_ref[i] = orth


def next_weight(fast, orth):
    return (fast - orth.astype(F32)).astype(BF16)


def second_kernel(core_ref, q_ref, g_ref, u_ref, d_ref, mine_ref, other_ref, out_ref):
    head = pl.program_id(0)
    low_core = core_ref[0] == 0
    nexts = []
    for mat, ref in enumerate((g_ref, u_ref, d_ref)):
        at = head * 3 + mat
        in_low = at < GROUP
        index = jnp.where(in_low, at, at - (GROUP - 1))
        orth = jnp.where(in_low == low_core, mine_ref[index], other_ref[index])
        nexts.append(next_weight(ref[0], orth))
    out_ref[...] = apply_fast(q_ref[0], *nexts)


def lay_first_kernel(place_ref, *refs):
    hop = pl.program_id(0)
    for i, ref in enumerate(refs[:-1]):

        @pl.when(hop == i)
        def _(ref=ref):
            refs[-1][0] = ref[...]


def lay_second_kernel(buf_ref, rows_ref, out_ref):
    out_ref[...] = rows_ref[...]


def local(queries, key_rows, value_rows, step_rates, gate_fast, up_fast, down_fast):
    rows = key_rows.shape[0]
    width = key_rows.shape[1]
    core = lax.axis_index("core").astype(jnp.int32).reshape(1)
    n_head = lax.axis_size("head")
    part = rows // n_head
    params = pltpu.CompilerParams(dimension_semantics=("arbitrary",), vmem_limit_bytes=VMEM_LIMIT)
    weight_spec = pl.BlockSpec((1, HD, HD), lambda h, *_: (h, 0, 0))
    rows_spec = pl.BlockSpec((rows, HD), lambda h, *_: (0, h))
    rows_shape = jax.ShapeDtypeStruct((rows, width), BF16)

    piece_shape = (GROUP, HD, HD)
    piece_spec = pl.BlockSpec(piece_shape, lambda h, c: (0, 0, 0))
    args = (queries, key_rows, value_rows, step_rates, gate_fast, up_fast, down_fast)
    q_hbm, k_hbm, v_hbm, rate_hbm, g_hbm, u_hbm, d_hbm = [
        pltpu.with_memory_space_constraint(x, pltpu.HBM) for x in args
    ]
    keep, send = pl.pallas_call(
        grad_kernel,
        grid_spec=pltpu.PrefetchScalarGridSpec(
            num_scalar_prefetch=1,
            grid=(HEADS_HERE,),
            in_specs=[
                rows_spec,
                rows_spec,
                pl.BlockSpec((HEADS_HERE, rows), lambda h, c: (0, 0)),
                weight_spec,
                weight_spec,
                weight_spec,
            ],
            out_specs=[piece_spec, piece_spec],
        ),
        out_shape=[jax.ShapeDtypeStruct(piece_shape, BF16), jax.ShapeDtypeStruct(piece_shape, BF16)],
        compiler_params=params,
        name="grads",
    )(core, k_hbm, v_hbm, rate_hbm, g_hbm, u_hbm, d_hbm)

    swap = [(0, 1), (1, 0)]
    received = lax.ppermute(send, "core", swap)
    place = lax.axis_index("head").astype(jnp.int32).reshape(1)
    part_spec = pl.BlockSpec((part, HD), lambda h, p: (0, h))
    firsts = pl.pallas_call(
        first_kernel,
        grid_spec=pltpu.PrefetchScalarGridSpec(
            num_scalar_prefetch=1,
            grid=(HEADS_HERE,),
            in_specs=[pl.BlockSpec((1, rows, HD), lambda h, p: (0, 0, h)), weight_spec, weight_spec, weight_spec],
            out_specs=[part_spec] * n_head,
            scratch_shapes=[pltpu.VMEM((rows, HD), BF16)],
        ),
        out_shape=[jax.ShapeDtypeStruct((part, width), BF16)] * n_head,
        compiler_params=params,
        name="first",
    )(place, q_hbm, g_hbm, u_hbm, d_hbm)
    firsts = [firsts[0]] + [
        lax.ppermute(firsts[hop], "head", [(i, (i + hop) % n_head) for i in range(n_head)])
        for hop in range(1, n_head)
    ]

    chip_sum = (keep.astype(F32) + received.astype(F32)).astype(BF16)
    slots = ("y", "z_lo")
    by_slot = lax.all_to_all(chip_sum, slots, split_axis=0, concat_axis=0, tiled=True)
    by_slot, *firsts = lax.optimization_barrier((by_slot, *firsts))
    partial = jnp.sum(by_slot.astype(F32), axis=0).astype(BF16)
    n_far = lax.axis_size("z_hi")
    partials = [partial] + [
        lax.ppermute(partial, "z_hi", [(i, (i + hop) % n_far) for i in range(n_far)]) for hop in range(1, n_far)
    ]
    orth = pl.pallas_call(
        orth_kernel,
        out_shape=jax.ShapeDtypeStruct(piece_shape, BF16),
        compiler_params=pltpu.CompilerParams(vmem_limit_bytes=VMEM_LIMIT),
        name="orthogonalize",
    )(*partials)
    orth_mine = lax.all_to_all(orth, slots, split_axis=0, concat_axis=0, tiled=True)
    orth_other = lax.ppermute(orth_mine, "core", swap)

    group_spec = pl.BlockSpec((GROUP, HD, HD), lambda h, c: (0, 0, 0))
    second = pl.pallas_call(
        second_kernel,
        grid_spec=pltpu.PrefetchScalarGridSpec(
            num_scalar_prefetch=1,
            grid=(HEADS_HERE,),
            in_specs=[pl.BlockSpec((1, rows, HD), lambda h, c: (1, 0, h))] + [weight_spec] * 3 + [group_spec] * 2,
            out_specs=rows_spec,
        ),
        out_shape=rows_shape,
        compiler_params=params,
        name="second",
    )(core, queries, gate_fast, up_fast, down_fast, orth_mine, orth_other)

    swapped = lax.all_to_all(second.reshape(n_head, part, width), "head", split_axis=0, concat_axis=0, tiled=True)
    out_shape = jax.ShapeDtypeStruct((2, part, n_head * width), BF16)
    out = pl.pallas_call(
        lay_first_kernel,
        grid_spec=pltpu.PrefetchScalarGridSpec(
            num_scalar_prefetch=1,
            grid=(n_head,),
            in_specs=[pl.BlockSpec((part, width), lambda s, p: (0, 0))] * n_head,
            out_specs=pl.BlockSpec((1, part, width), lambda s, p: (0, 0, lax.rem(p[0] + n_head - s, n_head))),
        ),
        out_shape=out_shape,
        compiler_params=params,
        name="lay_first",
    )(place, *firsts)
    return pl.pallas_call(
        lay_second_kernel,
        grid=(n_head,),
        in_specs=[
            pl.BlockSpec(memory_space=pl.ANY),
            pl.BlockSpec((1, part, width), lambda s: (s, 0, 0)),
        ],
        out_specs=pl.BlockSpec((1, part, width), lambda s: (1, 0, s)),
        out_shape=out_shape,
        input_output_aliases={0: 0},
        compiler_params=params,
        name="lay_second",
    )(out, swapped)


def solution(mesh):
    heads = mesh.shape["head"]
    fine = Mesh(mesh.devices.reshape(heads, 4, 2, 4, 2), ("head", "z_hi", "z_lo", "y", "core"))
    tok = ("z_hi", "z_lo", "y", "core")
    placed = (
        P(None, tok, "head"),
        P(tok, "head"),
        P(tok, "head"),
        P("head", tok),
        P("head", None, None),
        P("head", None, None),
        P("head", None, None),
    )
    return jax.shard_map(
        local, mesh=fine, in_specs=placed, out_specs=P(None, tok + ("head",), None), check_vma=False
    )
```

```python
import jax
import jax.numpy as jnp
from jax import lax
from jax.experimental import pallas as pl
from jax.experimental.pallas import tpu as pltpu
from jax.sharding import Mesh, PartitionSpec as P

NS_STEPS = 3
coef_first = 3.4445
coef_second = -4.775
coef_third = 2.0315
F32 = jnp.float32
BF16 = jnp.bfloat16
HD = 256
HALF = 128
HEADS_HERE = 5
MATS = 3 * HEADS_HERE
GROUP = 8
N_FAR = 4
VMEM_LIMIT = 48 * 1024 * 1024


def dot_f32(a, b):
    return lax.dot_general(a, b, (((1,), (0,)), ((), ())), preferred_element_type=F32)


def dot_nt(a, b):
    return lax.dot_general(a, b, (((1,), (1,)), ((), ())), preferred_element_type=F32)


def dot_tn(a, b):
    return lax.dot_general(a, b, (((0,), (0,)), ((), ())), preferred_element_type=F32)


def sigmoid(x):
    return 0.5 * jnp.tanh(0.5 * x) + 0.5


def apply_fast(rows, gate, up, down):
    zg = dot_f32(rows, gate)
    zu = dot_f32(rows, up)
    hidden = (zg * sigmoid(zg) * zu).astype(BF16)
    return dot_f32(hidden, down).astype(BF16)


def first_kernel(place_ref, q_ref, g_ref, u_ref, d_ref, *refs):
    out_refs, rows_ref = refs[:-1], refs[-1]
    weights = [ref[0].astype(BF16) for ref in (g_ref, u_ref, d_ref)]
    rows_ref[...] = apply_fast(q_ref[0], *weights)
    count = len(out_refs)
    part = rows_ref.shape[0] // count
    for hop, out_ref in enumerate(out_refs):
        to = lax.rem(place_ref[0] + hop, count)
        out_ref[...] = rows_ref[pl.ds(pl.multiple_of(to * part, part), part), :]


def twist_of(far_ref):
    return jnp.where(far_ref[0] >= N_FAR // 2, 1, 0)


def grad_kernel(core_ref, far_ref, k_ref, v_ref, rate_ref, g_ref, u_ref, d_ref, keep_ref, send_ref):
    head = pl.program_id(0)
    core = core_ref[0]
    twist = twist_of(far_ref)
    gate = g_ref[0].astype(BF16)
    up = u_ref[0].astype(BF16)
    down = d_ref[0].astype(BF16)
    keys = k_ref[...]
    zg = dot_f32(keys, gate)
    zu = dot_f32(keys, up)
    sig = sigmoid(zg)
    silu = zg * sig
    hidden = (silu * zu).astype(BF16)
    rate = rate_ref[pl.ds(head, 1), :]
    rate = jnp.transpose(jnp.broadcast_to(rate, (HALF, rate.shape[1])))
    rate = jnp.concatenate([rate, rate], axis=1)
    dout = (-(rate * v_ref[...].astype(F32))).astype(BF16)
    dh = dot_nt(dout, down)
    dzu = (dh * silu).astype(BF16)
    dzg = (dh * zu * sig * (1.0 + zg * (1.0 - sig))).astype(BF16)
    pair = dot_tn(keys, jnp.concatenate([dzg, dzu], axis=1)).astype(BF16)
    grads = (pair[:, :HD], pair[:, HD:], dot_tn(hidden, dout).astype(BF16))
    for mat in range(3):
        grad = grads[mat]
        at = head * 3 + mat
        for group in range(2):
            slot = at - group * (GROUP - 1)
            inside = (slot >= 0) & (slot < GROUP)
            for ref, wanted in ((keep_ref, core == group), (send_ref, core != group)):

                @pl.when(inside & wanted)
                def _(ref=ref, slot=slot, grad=grad):
                    ref[jnp.bitwise_xor(slot, twist)] = grad


def split(x):
    high = x.astype(BF16)
    return high, (x - high.astype(F32)).astype(BF16)


def orth_kernel(*refs):
    out_ref = refs[-1]
    m = refs[0][...].astype(F32)
    for ref in refs[1:-1]:
        m = m + ref[...].astype(F32)
    x = m / (jnp.sqrt(jnp.sum(m * m, keepdims=True)) + 1e-07)
    for sweep in range(NS_STEPS):
        if sweep < NS_STEPS - 1:
            low = x.astype(BF16)
            gram = dot_nt(low, low)
            half = gram.astype(BF16)
            poly = (coef_second * gram + coef_third * dot_f32(half, half)).astype(BF16)
            x = coef_first * x + dot_f32(poly, low)
        else:
            h, l = split(x)
            gram = dot_nt(h, h) + (dot_nt(h, l) + dot_nt(l, h))
            gh, gl = split(gram)
            square = dot_f32(gh, gh) + (dot_f32(gh, gl) + dot_f32(gl, gh))
            ph, pw = split(coef_second * gram + coef_third * square)
            x = coef_first * x + (dot_f32(ph, h) + (dot_f32(ph, l) + dot_f32(pw, h)))
    orth = x.astype(BF16)
    for i in range(out_ref.shape[0]):
        out_ref[i] = orth


def next_weight(fast, orth):
    return (fast - orth.astype(F32)).astype(BF16)


def second_kernel(core_ref, far_ref, q_ref, g_ref, u_ref, d_ref, mine_ref, other_ref, out_ref):
    head = pl.program_id(0)
    low_core = core_ref[0] == 0
    twist = twist_of(far_ref)
    nexts = []
    for mat, ref in enumerate((g_ref, u_ref, d_ref)):
        at = head * 3 + mat
        in_low = at < GROUP
        index = jnp.bitwise_xor(jnp.where(in_low, at, at - (GROUP - 1)), twist)
        orth = jnp.where(in_low == low_core, mine_ref[index], other_ref[index])
        nexts.append(next_weight(ref[0], orth))
    out_ref[...] = apply_fast(q_ref[0], *nexts)


def lay_first_kernel(place_ref, *refs):
    hop = pl.program_id(0)
    for i, ref in enumerate(refs[:-1]):

        @pl.when(hop == i)
        def _(ref=ref):
            refs[-1][0] = ref[...]


def lay_second_kernel(buf_ref, rows_ref, out_ref, sems):
    count, _, width = rows_ref.shape
    copies = [
        pltpu.make_async_copy(rows_ref.at[i], out_ref.at[1, :, pl.ds(i * width, width)], sems.at[i])
        for i in range(count)
    ]
    for copy in copies:
        copy.start()
    for copy in copies:
        copy.wait()


def local(queries, key_rows, value_rows, step_rates, gate_fast, up_fast, down_fast):
    rows = key_rows.shape[0]
    width = key_rows.shape[1]
    core = lax.axis_index("core").astype(jnp.int32).reshape(1)
    far = lax.axis_index("z_hi").astype(jnp.int32).reshape(1)
    n_head = lax.axis_size("head")
    part = rows // n_head
    params = pltpu.CompilerParams(dimension_semantics=("arbitrary",), vmem_limit_bytes=VMEM_LIMIT)
    weight_spec = pl.BlockSpec((1, HD, HD), lambda h, *_: (h, 0, 0))
    rows_spec = pl.BlockSpec((rows, HD), lambda h, *_: (0, h))
    rows_shape = jax.ShapeDtypeStruct((rows, width), BF16)

    piece_shape = (GROUP, HD, HD)
    piece_spec = pl.BlockSpec(piece_shape, lambda h, *_: (0, 0, 0))
    args = (queries, key_rows, value_rows, step_rates, gate_fast, up_fast, down_fast)
    q_hbm, k_hbm, v_hbm, rate_hbm, g_hbm, u_hbm, d_hbm = [
        pltpu.with_memory_space_constraint(x, pltpu.HBM) for x in args
    ]
    keep, send = pl.pallas_call(
        grad_kernel,
        grid_spec=pltpu.PrefetchScalarGridSpec(
            num_scalar_prefetch=2,
            grid=(HEADS_HERE,),
            in_specs=[
                rows_spec,
                rows_spec,
                pl.BlockSpec((HEADS_HERE, rows), lambda h, *_: (0, 0)),
                weight_spec,
                weight_spec,
                weight_spec,
            ],
            out_specs=[piece_spec, piece_spec],
        ),
        out_shape=[jax.ShapeDtypeStruct(piece_shape, BF16), jax.ShapeDtypeStruct(piece_shape, BF16)],
        compiler_params=params,
        name="grads",
    )(core, far, k_hbm, v_hbm, rate_hbm, g_hbm, u_hbm, d_hbm)

    swap = [(0, 1), (1, 0)]
    received = lax.ppermute(send, "core", swap)
    place = lax.axis_index("head").astype(jnp.int32).reshape(1)
    part_spec = pl.BlockSpec((part, HD), lambda h, p: (0, h))
    firsts = pl.pallas_call(
        first_kernel,
        grid_spec=pltpu.PrefetchScalarGridSpec(
            num_scalar_prefetch=1,
            grid=(HEADS_HERE,),
            in_specs=[pl.BlockSpec((1, rows, HD), lambda h, p: (0, 0, h)), weight_spec, weight_spec, weight_spec],
            out_specs=[part_spec] * n_head,
            scratch_shapes=[pltpu.VMEM((rows, HD), BF16)],
        ),
        out_shape=[jax.ShapeDtypeStruct((part, width), BF16)] * n_head,
        compiler_params=params,
        name="first",
    )(place, q_hbm, g_hbm, u_hbm, d_hbm)
    firsts = [firsts[0]] + [
        lax.ppermute(firsts[hop], "head", [(i, (i + hop) % n_head) for i in range(n_head)])
        for hop in range(1, n_head)
    ]

    chip_sum = (keep.astype(F32) + received.astype(F32)).astype(BF16)
    slots = ("y", "z_lo")
    by_slot = lax.all_to_all(chip_sum, slots, split_axis=0, concat_axis=0, tiled=True)
    partial = jnp.sum(by_slot.astype(F32), axis=0).astype(BF16)
    rings = [[2 * i + (slot ^ (i >= N_FAR // 2)) for i in range(N_FAR)] for slot in range(2)]
    partials = [partial] + [
        lax.ppermute(
            partial, ("z_hi", "z_lo"), [(ring[i], ring[(i + hop) % N_FAR]) for ring in rings for i in range(N_FAR)]
        )
        for hop in range(1, N_FAR)
    ]
    late = lax.optimization_barrier((*partials, *firsts))
    partials, firsts = late[:N_FAR], late[N_FAR:]
    orth = pl.pallas_call(
        orth_kernel,
        out_shape=jax.ShapeDtypeStruct(piece_shape, BF16),
        compiler_params=pltpu.CompilerParams(vmem_limit_bytes=VMEM_LIMIT),
        name="orthogonalize",
    )(*partials)
    orth_mine = lax.all_to_all(orth, slots, split_axis=0, concat_axis=0, tiled=True)
    orth_other = lax.ppermute(orth_mine, "core", swap)

    group_spec = pl.BlockSpec((GROUP, HD, HD), lambda h, *_: (0, 0, 0))
    second = pl.pallas_call(
        second_kernel,
        grid_spec=pltpu.PrefetchScalarGridSpec(
            num_scalar_prefetch=2,
            grid=(HEADS_HERE,),
            in_specs=[pl.BlockSpec((1, rows, HD), lambda h, *_: (1, 0, h))] + [weight_spec] * 3 + [group_spec] * 2,
            out_specs=rows_spec,
        ),
        out_shape=rows_shape,
        compiler_params=params,
        name="second",
    )(core, far, queries, gate_fast, up_fast, down_fast, orth_mine, orth_other)

    swapped = lax.all_to_all(second.reshape(n_head, part, width), "head", split_axis=0, concat_axis=0, tiled=True)
    out_shape = jax.ShapeDtypeStruct((2, part, n_head * width), BF16)
    out = pl.pallas_call(
        lay_first_kernel,
        grid_spec=pltpu.PrefetchScalarGridSpec(
            num_scalar_prefetch=1,
            grid=(n_head,),
            in_specs=[pl.BlockSpec((part, width), lambda s, p: (0, 0))] * n_head,
            out_specs=pl.BlockSpec((1, part, width), lambda s, p: (0, 0, lax.rem(p[0] + n_head - s, n_head))),
        ),
        out_shape=out_shape,
        compiler_params=params,
        name="lay_first",
    )(place, *firsts)
    return pl.pallas_call(
        lay_second_kernel,
        in_specs=[pl.BlockSpec(memory_space=pl.ANY), pl.BlockSpec(memory_space=pltpu.VMEM)],
        out_specs=pl.BlockSpec(memory_space=pl.ANY),
        out_shape=out_shape,
        input_output_aliases={0: 0},
        scratch_shapes=[pltpu.SemaphoreType.DMA((n_head,))],
        name="lay_second",
    )(out, swapped)


def solution(mesh):
    heads = mesh.shape["head"]
    fine = Mesh(mesh.devices.reshape(heads, 4, 2, 4, 2), ("head", "z_hi", "z_lo", "y", "core"))
    tok = ("z_hi", "z_lo", "y", "core")
    placed = (
        P(None, tok, "head"),
        P(tok, "head"),
        P(tok, "head"),
        P("head", tok),
        P("head", None, None),
        P("head", None, None),
        P("head", None, None),
    )
    return jax.shard_map(
        local, mesh=fine, in_specs=placed, out_specs=P(None, tok + ("head",), None), check_vma=False
    )
```

```python
import jax
import jax.numpy as jnp
from jax import lax
from jax.experimental import pallas as pl
from jax.experimental.pallas import tpu as pltpu
from jax.sharding import Mesh, PartitionSpec as P

NS_STEPS = 3
coef_first = 3.4445
coef_second = -4.775
coef_third = 2.0315
F32 = jnp.float32
BF16 = jnp.bfloat16
HD = 256
HALF = 128
HEADS_HERE = 5
MATS = 3 * HEADS_HERE
GROUP = 8
N_FAR = 4
VMEM_LIMIT = 48 * 1024 * 1024


def dot_f32(a, b):
    return lax.dot_general(a, b, (((1,), (0,)), ((), ())), preferred_element_type=F32)


def dot_nt(a, b):
    return lax.dot_general(a, b, (((1,), (1,)), ((), ())), preferred_element_type=F32)


def dot_tn(a, b):
    return lax.dot_general(a, b, (((0,), (0,)), ((), ())), preferred_element_type=F32)


def sigmoid(x):
    return 0.5 * jnp.tanh(0.5 * x) + 0.5


def apply_fast(rows, gate, up, down):
    zg = dot_f32(rows, gate)
    zu = dot_f32(rows, up)
    hidden = (zg * sigmoid(zg) * zu).astype(BF16)
    return dot_f32(hidden, down).astype(BF16)


def first_kernel(place_ref, q_ref, g_ref, u_ref, d_ref, *refs):
    out_refs, rows_ref = refs[:-1], refs[-1]
    weights = [ref[0].astype(BF16) for ref in (g_ref, u_ref, d_ref)]
    rows_ref[...] = apply_fast(q_ref[0], *weights)
    count = len(out_refs)
    part = rows_ref.shape[0] // count
    for hop, out_ref in enumerate(out_refs):
        to = lax.rem(place_ref[0] + hop, count)
        out_ref[...] = rows_ref[pl.ds(pl.multiple_of(to * part, part), part), :]


def twist_of(far_ref):
    return jnp.where(far_ref[0] >= N_FAR // 2, 1, 0)


def grad_kernel(core_ref, far_ref, k_ref, v_ref, rate_ref, g_ref, u_ref, d_ref, keep_ref, send_ref, *scratch):
    rates, keys, values, gates, ups, downs, rate_sem, sems = scratch
    twist = twist_of(far_ref)
    rate_copy = pltpu.make_async_copy(rate_ref, rates, rate_sem)
    rate_copy.start()
    copies = []
    for head in range(HEADS_HERE):
        cols = pl.ds(head * HD, HD)
        pairs = (
            (k_ref.at[:, cols], keys),
            (v_ref.at[:, cols], values),
            (g_ref.at[head], gates),
            (u_ref.at[head], ups),
            (d_ref.at[head], downs),
        )
        copies.append([pltpu.make_async_copy(src, dst.at[head], sems.at[head, i]) for i, (src, dst) in enumerate(pairs)])
        for copy in copies[-1]:
            copy.start()
    rate_copy.wait()

    def all_heads(group_refs):
        for head in range(HEADS_HERE):
            for copy in copies[head]:
                copy.wait()
            grads = head_grads(
                keys[head],
                values[head],
                rates[head : head + 1, :],
                gates[head].astype(BF16),
                ups[head].astype(BF16),
                downs[head].astype(BF16),
            )
            for mat, grad in enumerate(grads):
                for group, ref in enumerate(group_refs):
                    slot = head * 3 + mat - group * (GROUP - 1)
                    if 0 <= slot < GROUP:
                        ref[jnp.bitwise_xor(slot, twist)] = grad

    @pl.when(core_ref[0] == 0)
    def _():
        all_heads((keep_ref, send_ref))

    @pl.when(core_ref[0] != 0)
    def _():
        all_heads((send_ref, keep_ref))


def head_grads(keys, values, rate, gate, up, down):
    zg = dot_f32(keys, gate)
    zu = dot_f32(keys, up)
    sig = sigmoid(zg)
    silu = zg * sig
    hidden = (silu * zu).astype(BF16)
    rate = jnp.transpose(jnp.broadcast_to(rate, (HALF, rate.shape[1])))
    rate = jnp.concatenate([rate, rate], axis=1)
    dout = (-(rate * values.astype(F32))).astype(BF16)
    dh = dot_nt(dout, down)
    dzu = (dh * silu).astype(BF16)
    dzg = (dh * zu * sig * (1.0 + zg * (1.0 - sig))).astype(BF16)
    pair = dot_tn(keys, jnp.concatenate([dzg, dzu], axis=1)).astype(BF16)
    return pair[:, :HD], pair[:, HD:], dot_tn(hidden, dout).astype(BF16)


def split(x):
    high = x.astype(BF16)
    return high, (x - high.astype(F32)).astype(BF16)


def orth_kernel(*refs):
    out_ref = refs[-1]
    m = refs[0][...].astype(F32)
    for ref in refs[1:-1]:
        m = m + ref[...].astype(F32)
    x = m / (jnp.sqrt(jnp.sum(m * m, keepdims=True)) + 1e-07)
    for sweep in range(NS_STEPS):
        if sweep < NS_STEPS - 1:
            low = x.astype(BF16)
            gram = dot_nt(low, low)
            half = gram.astype(BF16)
            poly = (coef_second * gram + coef_third * dot_f32(half, half)).astype(BF16)
            x = coef_first * x + dot_f32(poly, low)
        else:
            h, l = split(x)
            gram = dot_nt(h, h) + (dot_nt(h, l) + dot_nt(l, h))
            gh, gl = split(gram)
            square = dot_f32(gh, gh) + (dot_f32(gh, gl) + dot_f32(gl, gh))
            ph, pw = split(coef_second * gram + coef_third * square)
            x = coef_first * x + (dot_f32(ph, h) + (dot_f32(ph, l) + dot_f32(pw, h)))
    orth = x.astype(BF16)
    for i in range(out_ref.shape[0]):
        out_ref[i] = orth


def next_weight(fast, orth):
    return (fast - orth.astype(F32)).astype(BF16)


def second_kernel(core_ref, far_ref, q_ref, g_ref, u_ref, d_ref, mine_ref, other_ref, out_ref):
    low_core = core_ref[0] == 0
    twist = twist_of(far_ref)
    for head in range(HEADS_HERE):
        nexts = []
        for mat, ref in enumerate((g_ref, u_ref, d_ref)):
            at = head * 3 + mat
            in_low = at < GROUP
            index = jnp.bitwise_xor(at if in_low else at - (GROUP - 1), twist)
            pair = (mine_ref[index], other_ref[index])
            orth = jnp.where(low_core, *(pair if in_low else pair[::-1]))
            nexts.append(next_weight(ref[head], orth))
        cols = slice(head * HD, (head + 1) * HD)
        out_ref[:, cols] = apply_fast(q_ref[0, :, cols], *nexts)


def lay_first_kernel(place_ref, *refs):
    hop = pl.program_id(0)
    for i, ref in enumerate(refs[:-1]):

        @pl.when(hop == i)
        def _(ref=ref):
            refs[-1][0] = ref[...]


def lay_second_kernel(buf_ref, rows_ref, out_ref):
    out_ref[...] = rows_ref[...]


def local(queries, key_rows, value_rows, step_rates, gate_fast, up_fast, down_fast):
    rows = key_rows.shape[0]
    width = key_rows.shape[1]
    core = lax.axis_index("core").astype(jnp.int32).reshape(1)
    far = lax.axis_index("z_hi").astype(jnp.int32).reshape(1)
    n_head = lax.axis_size("head")
    part = rows // n_head
    params = pltpu.CompilerParams(dimension_semantics=("arbitrary",), vmem_limit_bytes=VMEM_LIMIT)
    weight_spec = pl.BlockSpec((1, HD, HD), lambda h, *_: (h, 0, 0))
    rows_shape = jax.ShapeDtypeStruct((rows, width), BF16)

    piece_shape = (GROUP, HD, HD)
    piece_spec = pl.BlockSpec(piece_shape, lambda h, *_: (0, 0, 0))
    args = (queries, key_rows, value_rows, step_rates, gate_fast, up_fast, down_fast)
    q_hbm, k_hbm, v_hbm, rate_hbm, g_hbm, u_hbm, d_hbm = [
        pltpu.with_memory_space_constraint(x, pltpu.HBM) for x in args
    ]
    any_spec = pl.BlockSpec(memory_space=pl.ANY)
    keep, send = pl.pallas_call(
        grad_kernel,
        grid_spec=pltpu.PrefetchScalarGridSpec(
            num_scalar_prefetch=2,
            grid=(1,),
            in_specs=[any_spec] * 6,
            out_specs=[piece_spec, piece_spec],
            scratch_shapes=[
                pltpu.VMEM((HEADS_HERE, rows), F32),
                pltpu.VMEM((HEADS_HERE, rows, HD), BF16),
                pltpu.VMEM((HEADS_HERE, rows, HD), BF16),
                pltpu.VMEM((HEADS_HERE, HD, HD), F32),
                pltpu.VMEM((HEADS_HERE, HD, HD), F32),
                pltpu.VMEM((HEADS_HERE, HD, HD), F32),
                pltpu.SemaphoreType.DMA(()),
                pltpu.SemaphoreType.DMA((HEADS_HERE, 5)),
            ],
        ),
        out_shape=[jax.ShapeDtypeStruct(piece_shape, BF16), jax.ShapeDtypeStruct(piece_shape, BF16)],
        compiler_params=params,
        name="grads",
    )(core, far, k_hbm, v_hbm, rate_hbm, g_hbm, u_hbm, d_hbm)

    swap = [(0, 1), (1, 0)]
    received = lax.ppermute(send, "core", swap)
    place = lax.axis_index("head").astype(jnp.int32).reshape(1)
    part_spec = pl.BlockSpec((part, HD), lambda h, p: (0, h))
    firsts = pl.pallas_call(
        first_kernel,
        grid_spec=pltpu.PrefetchScalarGridSpec(
            num_scalar_prefetch=1,
            grid=(HEADS_HERE,),
            in_specs=[pl.BlockSpec((1, rows, HD), lambda h, p: (0, 0, h)), weight_spec, weight_spec, weight_spec],
            out_specs=[part_spec] * n_head,
            scratch_shapes=[pltpu.VMEM((rows, HD), BF16)],
        ),
        out_shape=[jax.ShapeDtypeStruct((part, width), BF16)] * n_head,
        compiler_params=params,
        name="first",
    )(place, q_hbm, g_hbm, u_hbm, d_hbm)
    firsts = [firsts[0]] + [
        lax.ppermute(firsts[hop], "head", [(i, (i + hop) % n_head) for i in range(n_head)])
        for hop in range(1, n_head)
    ]

    chip_sum = (keep.astype(F32) + received.astype(F32)).astype(BF16)
    slots = ("y", "z_lo")
    by_slot = lax.all_to_all(chip_sum, slots, split_axis=0, concat_axis=0, tiled=True)
    partial = jnp.sum(by_slot.astype(F32), axis=0).astype(BF16)
    rings = [[2 * i + (slot ^ (i >= N_FAR // 2)) for i in range(N_FAR)] for slot in range(2)]
    partials = [partial] + [
        lax.ppermute(
            partial, ("z_hi", "z_lo"), [(ring[i], ring[(i + hop) % N_FAR]) for ring in rings for i in range(N_FAR)]
        )
        for hop in range(1, N_FAR)
    ]
    late = lax.optimization_barrier((*partials, *firsts))
    partials, firsts = late[:N_FAR], late[N_FAR:]
    orth = pl.pallas_call(
        orth_kernel,
        out_shape=jax.ShapeDtypeStruct(piece_shape, BF16),
        compiler_params=pltpu.CompilerParams(vmem_limit_bytes=VMEM_LIMIT),
        name="orthogonalize",
    )(*partials)
    orth_mine = lax.all_to_all(orth, slots, split_axis=0, concat_axis=0, tiled=True)
    orth_other = lax.ppermute(orth_mine, "core", swap)

    group_spec = pl.BlockSpec((GROUP, HD, HD), lambda i, *_: (0, 0, 0))
    fast_spec = pl.BlockSpec((HEADS_HERE, HD, HD), lambda i, *_: (0, 0, 0))
    second = pl.pallas_call(
        second_kernel,
        grid_spec=pltpu.PrefetchScalarGridSpec(
            num_scalar_prefetch=2,
            grid=(1,),
            in_specs=[pl.BlockSpec((1, rows, width), lambda i, *_: (1, 0, 0))] + [fast_spec] * 3 + [group_spec] * 2,
            out_specs=pl.BlockSpec((rows, width), lambda i, *_: (0, 0)),
        ),
        out_shape=rows_shape,
        compiler_params=params,
        name="second",
    )(core, far, queries, gate_fast, up_fast, down_fast, orth_mine, orth_other)

    swapped = lax.all_to_all(second.reshape(n_head, part, width), "head", split_axis=0, concat_axis=0, tiled=True)
    out_shape = jax.ShapeDtypeStruct((2, part, n_head * width), BF16)
    out = pl.pallas_call(
        lay_first_kernel,
        grid_spec=pltpu.PrefetchScalarGridSpec(
            num_scalar_prefetch=1,
            grid=(n_head,),
            in_specs=[pl.BlockSpec((part, width), lambda s, p: (0, 0))] * n_head,
            out_specs=pl.BlockSpec((1, part, width), lambda s, p: (0, 0, lax.rem(p[0] + n_head - s, n_head))),
        ),
        out_shape=out_shape,
        compiler_params=params,
        name="lay_first",
    )(place, *firsts)
    return pl.pallas_call(
        lay_second_kernel,
        grid=(n_head,),
        in_specs=[
            pl.BlockSpec(memory_space=pl.ANY),
            pl.BlockSpec((1, part, width), lambda s: (s, 0, 0)),
        ],
        out_specs=pl.BlockSpec((1, part, width), lambda s: (1, 0, s)),
        out_shape=out_shape,
        input_output_aliases={0: 0},
        compiler_params=params,
        name="lay_second",
    )(out, swapped)


def solution(mesh):
    heads = mesh.shape["head"]
    fine = Mesh(mesh.devices.reshape(heads, 4, 2, 4, 2), ("head", "z_hi", "z_lo", "y", "core"))
    tok = ("z_hi", "z_lo", "y", "core")
    placed = (
        P(None, tok, "head"),
        P(tok, "head"),
        P(tok, "head"),
        P("head", tok),
        P("head", None, None),
        P("head", None, None),
        P("head", None, None),
    )
    return jax.shard_map(
        local, mesh=fine, in_specs=placed, out_specs=P(None, tok + ("head",), None), check_vma=False
    )
```

```python
import jax
import jax.numpy as jnp
from jax import lax
from jax.experimental import pallas as pl
from jax.experimental.pallas import tpu as pltpu
from jax.sharding import Mesh, PartitionSpec as P

NS_STEPS = 3
coef_first = 3.4445
coef_second = -4.775
coef_third = 2.0315
F32 = jnp.float32
BF16 = jnp.bfloat16
HD = 256
HALF = 128
HEADS_HERE = 5
MATS = 3 * HEADS_HERE
GROUP = 8
N_FAR = 4
VMEM_LIMIT = 48 * 1024 * 1024


def dot_f32(a, b):
    return lax.dot_general(a, b, (((1,), (0,)), ((), ())), preferred_element_type=F32)


def dot_nt(a, b):
    return lax.dot_general(a, b, (((1,), (1,)), ((), ())), preferred_element_type=F32)


def dot_tn(a, b):
    return lax.dot_general(a, b, (((0,), (0,)), ((), ())), preferred_element_type=F32)


def sigmoid(x):
    return 0.5 * jnp.tanh(0.5 * x) + 0.5


def apply_fast(rows, gate, up, down):
    zg = dot_f32(rows, gate)
    zu = dot_f32(rows, up)
    hidden = (zg * sigmoid(zg) * zu).astype(BF16)
    return dot_f32(hidden, down).astype(BF16)


def first_kernel(place_ref, q_ref, g_ref, u_ref, d_ref, *refs):
    out_refs, rows_ref = refs[:-1], refs[-1]
    weights = [ref[0].astype(BF16) for ref in (g_ref, u_ref, d_ref)]
    rows_ref[...] = apply_fast(q_ref[0], *weights)
    count = len(out_refs)
    part = rows_ref.shape[0] // count
    for hop, out_ref in enumerate(out_refs):
        to = lax.rem(place_ref[0] + hop, count)
        out_ref[...] = rows_ref[pl.ds(pl.multiple_of(to * part, part), part), :]


def twist_of(far_ref):
    return jnp.where(far_ref[0] >= N_FAR // 2, 1, 0)


def heads_of(heads, in_refs, scratch):
    k_ref, v_ref, rate_ref, g_ref, u_ref, d_ref = in_refs
    rates, keys, values, gates, ups, downs, rate_sem, sems = scratch
    rate_copy = pltpu.make_async_copy(rate_ref, rates, rate_sem)
    rate_copy.start()
    copies = []
    for at, head in enumerate(heads):
        cols = pl.ds(head * HD, HD)
        pairs = (
            (k_ref.at[:, cols], keys),
            (v_ref.at[:, cols], values),
            (g_ref.at[head], gates),
            (u_ref.at[head], ups),
            (d_ref.at[head], downs),
        )
        copies.append([pltpu.make_async_copy(src, dst.at[at], sems.at[at, i]) for i, (src, dst) in enumerate(pairs)])
        for copy in copies[-1]:
            copy.start()
    rate_copy.wait()
    for at, head in enumerate(heads):
        for copy in copies[at]:
            copy.wait()
        yield (
            head,
            head_grads(
                keys[at],
                values[at],
                rates[head : head + 1, :],
                gates[at].astype(BF16),
                ups[at].astype(BF16),
                downs[at].astype(BF16),
            ),
        )


def sent_kernel(core_ref, far_ref, *refs):
    in_refs, (send_ref, shared_ref), scratch = refs[:6], refs[6:8], refs[8:]
    twist = twist_of(far_ref)

    def run(heads, send_from, keep_from):
        for head, grads in heads_of(heads, in_refs, scratch):
            for mat, grad in enumerate(grads):
                at = head * 3 + mat
                if 0 <= at - send_from < GROUP:
                    send_ref[jnp.bitwise_xor(at - send_from, twist)] = grad
                if 0 <= at - keep_from < 2:
                    shared_ref[at - keep_from] = grad

    @pl.when(core_ref[0] == 0)
    def _():
        run((2, 3, 4), GROUP - 1, 6)

    @pl.when(core_ref[0] != 0)
    def _():
        run((0, 1, 2), 0, GROUP - 1)


def kept_kernel(core_ref, far_ref, *refs):
    in_refs, shared_ref, keep_ref, scratch = refs[:6], refs[6], refs[7], refs[8:]
    twist = twist_of(far_ref)

    def run(heads, keep_from, shared_from):
        for i in range(2):
            keep_ref[jnp.bitwise_xor(shared_from - keep_from + i, twist)] = shared_ref[i]
        for head, grads in heads_of(heads, in_refs, scratch):
            for mat, grad in enumerate(grads):
                keep_ref[jnp.bitwise_xor(head * 3 + mat - keep_from, twist)] = grad

    @pl.when(core_ref[0] == 0)
    def _():
        run((0, 1), 0, 6)

    @pl.when(core_ref[0] != 0)
    def _():
        run((3, 4), GROUP - 1, GROUP - 1)


def head_grads(keys, values, rate, gate, up, down):
    zg = dot_f32(keys, gate)
    zu = dot_f32(keys, up)
    sig = sigmoid(zg)
    silu = zg * sig
    hidden = (silu * zu).astype(BF16)
    rate = jnp.transpose(jnp.broadcast_to(rate, (HALF, rate.shape[1])))
    rate = jnp.concatenate([rate, rate], axis=1)
    dout = (-(rate * values.astype(F32))).astype(BF16)
    dh = dot_nt(dout, down)
    dzu = (dh * silu).astype(BF16)
    dzg = (dh * zu * sig * (1.0 + zg * (1.0 - sig))).astype(BF16)
    pair = dot_tn(keys, jnp.concatenate([dzg, dzu], axis=1)).astype(BF16)
    return pair[:, :HD], pair[:, HD:], dot_tn(hidden, dout).astype(BF16)


def split(x):
    high = x.astype(BF16)
    return high, (x - high.astype(F32)).astype(BF16)


def orth_kernel(*refs):
    out_ref = refs[-1]
    m = refs[0][...].astype(F32)
    for ref in refs[1:-1]:
        m = m + ref[...].astype(F32)
    x = m / (jnp.sqrt(jnp.sum(m * m, keepdims=True)) + 1e-07)
    for sweep in range(NS_STEPS):
        if sweep < NS_STEPS - 1:
            low = x.astype(BF16)
            gram = dot_nt(low, low)
            half = gram.astype(BF16)
            poly = (coef_second * gram + coef_third * dot_f32(half, half)).astype(BF16)
            x = coef_first * x + dot_f32(poly, low)
        else:
            h, l = split(x)
            gram = dot_nt(h, h) + (dot_nt(h, l) + dot_nt(l, h))
            gh, gl = split(gram)
            square = dot_f32(gh, gh) + (dot_f32(gh, gl) + dot_f32(gl, gh))
            ph, pw = split(coef_second * gram + coef_third * square)
            x = coef_first * x + (dot_f32(ph, h) + (dot_f32(ph, l) + dot_f32(pw, h)))
    orth = x.astype(BF16)
    for i in range(out_ref.shape[0]):
        out_ref[i] = orth


def next_weight(fast, orth):
    return (fast - orth.astype(F32)).astype(BF16)


def second_kernel(core_ref, far_ref, q_ref, g_ref, u_ref, d_ref, mine_ref, other_ref, out_ref):
    low_core = core_ref[0] == 0
    twist = twist_of(far_ref)
    for head in range(HEADS_HERE):
        nexts = []
        for mat, ref in enumerate((g_ref, u_ref, d_ref)):
            at = head * 3 + mat
            in_low = at < GROUP
            index = jnp.bitwise_xor(at if in_low else at - (GROUP - 1), twist)
            pair = (mine_ref[index], other_ref[index])
            orth = jnp.where(low_core, *(pair if in_low else pair[::-1]))
            nexts.append(next_weight(ref[head], orth))
        cols = slice(head * HD, (head + 1) * HD)
        out_ref[:, cols] = apply_fast(q_ref[0, :, cols], *nexts)


def lay_first_kernel(place_ref, *refs):
    hop = pl.program_id(0)
    for i, ref in enumerate(refs[:-1]):

        @pl.when(hop == i)
        def _(ref=ref):
            refs[-1][0] = ref[...]


def lay_second_kernel(buf_ref, rows_ref, out_ref):
    out_ref[...] = rows_ref[...]


def local(queries, key_rows, value_rows, step_rates, gate_fast, up_fast, down_fast):
    rows = key_rows.shape[0]
    width = key_rows.shape[1]
    core = lax.axis_index("core").astype(jnp.int32).reshape(1)
    far = lax.axis_index("z_hi").astype(jnp.int32).reshape(1)
    n_head = lax.axis_size("head")
    part = rows // n_head
    params = pltpu.CompilerParams(dimension_semantics=("arbitrary",), vmem_limit_bytes=VMEM_LIMIT)
    weight_spec = pl.BlockSpec((1, HD, HD), lambda h, *_: (h, 0, 0))
    rows_shape = jax.ShapeDtypeStruct((rows, width), BF16)

    piece_shape = (GROUP, HD, HD)
    piece_spec = pl.BlockSpec(piece_shape, lambda h, *_: (0, 0, 0))
    args = (queries, key_rows, value_rows, step_rates, gate_fast, up_fast, down_fast)
    q_hbm, k_hbm, v_hbm, rate_hbm, g_hbm, u_hbm, d_hbm = [
        pltpu.with_memory_space_constraint(x, pltpu.HBM) for x in args
    ]
    any_spec = pl.BlockSpec(memory_space=pl.ANY)
    piece_array = jax.ShapeDtypeStruct(piece_shape, BF16)
    shared_shape = (2, HD, HD)
    shared_spec = pl.BlockSpec(shared_shape, lambda h, *_: (0, 0, 0))

    def copy_scratch(heads):
        return [
            pltpu.VMEM((HEADS_HERE, rows), F32),
            pltpu.VMEM((heads, rows, HD), BF16),
            pltpu.VMEM((heads, rows, HD), BF16),
            pltpu.VMEM((heads, HD, HD), F32),
            pltpu.VMEM((heads, HD, HD), F32),
            pltpu.VMEM((heads, HD, HD), F32),
            pltpu.SemaphoreType.DMA(()),
            pltpu.SemaphoreType.DMA((heads, 5)),
        ]

    grad_inputs = (k_hbm, v_hbm, rate_hbm, g_hbm, u_hbm, d_hbm)
    send, shared = pl.pallas_call(
        sent_kernel,
        grid_spec=pltpu.PrefetchScalarGridSpec(
            num_scalar_prefetch=2,
            grid=(1,),
            in_specs=[any_spec] * 6,
            out_specs=[piece_spec, shared_spec],
            scratch_shapes=copy_scratch(3),
        ),
        out_shape=[piece_array, jax.ShapeDtypeStruct(shared_shape, BF16)],
        compiler_params=params,
        name="grads_sent",
    )(core, far, *grad_inputs)

    swap = [(0, 1), (1, 0)]
    received = lax.ppermute(send, "core", swap)
    keep = pl.pallas_call(
        kept_kernel,
        grid_spec=pltpu.PrefetchScalarGridSpec(
            num_scalar_prefetch=2,
            grid=(1,),
            in_specs=[any_spec] * 6 + [shared_spec],
            out_specs=piece_spec,
            scratch_shapes=copy_scratch(2),
        ),
        out_shape=piece_array,
        compiler_params=params,
        name="grads_kept",
    )(core, far, *grad_inputs, shared)
    place = lax.axis_index("head").astype(jnp.int32).reshape(1)
    part_spec = pl.BlockSpec((part, HD), lambda h, p: (0, h))
    firsts = pl.pallas_call(
        first_kernel,
        grid_spec=pltpu.PrefetchScalarGridSpec(
            num_scalar_prefetch=1,
            grid=(HEADS_HERE,),
            in_specs=[pl.BlockSpec((1, rows, HD), lambda h, p: (0, 0, h)), weight_spec, weight_spec, weight_spec],
            out_specs=[part_spec] * n_head,
            scratch_shapes=[pltpu.VMEM((rows, HD), BF16)],
        ),
        out_shape=[jax.ShapeDtypeStruct((part, width), BF16)] * n_head,
        compiler_params=params,
        name="first",
    )(place, q_hbm, g_hbm, u_hbm, d_hbm)
    firsts = [firsts[0]] + [
        lax.ppermute(firsts[hop], "head", [(i, (i + hop) % n_head) for i in range(n_head)])
        for hop in range(1, n_head)
    ]

    chip_sum = (keep.astype(F32) + received.astype(F32)).astype(BF16)
    slots = ("y", "z_lo")
    by_slot = lax.all_to_all(chip_sum, slots, split_axis=0, concat_axis=0, tiled=True)
    partial = jnp.sum(by_slot.astype(F32), axis=0).astype(BF16)
    rings = [[2 * i + (slot ^ (i >= N_FAR // 2)) for i in range(N_FAR)] for slot in range(2)]
    partials = [partial] + [
        lax.ppermute(
            partial, ("z_hi", "z_lo"), [(ring[i], ring[(i + hop) % N_FAR]) for ring in rings for i in range(N_FAR)]
        )
        for hop in range(1, N_FAR)
    ]
    late = lax.optimization_barrier((*partials, *firsts))
    partials, firsts = late[:N_FAR], late[N_FAR:]
    orth = pl.pallas_call(
        orth_kernel,
        out_shape=jax.ShapeDtypeStruct(piece_shape, BF16),
        compiler_params=pltpu.CompilerParams(vmem_limit_bytes=VMEM_LIMIT),
        name="orthogonalize",
    )(*partials)
    orth_mine = lax.all_to_all(orth, slots, split_axis=0, concat_axis=0, tiled=True)
    orth_other = lax.ppermute(orth_mine, "core", swap)

    group_spec = pl.BlockSpec((GROUP, HD, HD), lambda i, *_: (0, 0, 0))
    fast_spec = pl.BlockSpec((HEADS_HERE, HD, HD), lambda i, *_: (0, 0, 0))
    second = pl.pallas_call(
        second_kernel,
        grid_spec=pltpu.PrefetchScalarGridSpec(
            num_scalar_prefetch=2,
            grid=(1,),
            in_specs=[pl.BlockSpec((1, rows, width), lambda i, *_: (1, 0, 0))] + [fast_spec] * 3 + [group_spec] * 2,
            out_specs=pl.BlockSpec((rows, width), lambda i, *_: (0, 0)),
        ),
        out_shape=rows_shape,
        compiler_params=params,
        name="second",
    )(core, far, queries, gate_fast, up_fast, down_fast, orth_mine, orth_other)

    swapped = lax.all_to_all(second.reshape(n_head, part, width), "head", split_axis=0, concat_axis=0, tiled=True)
    out_shape = jax.ShapeDtypeStruct((2, part, n_head * width), BF16)
    out = pl.pallas_call(
        lay_first_kernel,
        grid_spec=pltpu.PrefetchScalarGridSpec(
            num_scalar_prefetch=1,
            grid=(n_head,),
            in_specs=[pl.BlockSpec((part, width), lambda s, p: (0, 0))] * n_head,
            out_specs=pl.BlockSpec((1, part, width), lambda s, p: (0, 0, lax.rem(p[0] + n_head - s, n_head))),
        ),
        out_shape=out_shape,
        compiler_params=params,
        name="lay_first",
    )(place, *firsts)
    return pl.pallas_call(
        lay_second_kernel,
        grid=(n_head,),
        in_specs=[
            pl.BlockSpec(memory_space=pl.ANY),
            pl.BlockSpec((1, part, width), lambda s: (s, 0, 0)),
        ],
        out_specs=pl.BlockSpec((1, part, width), lambda s: (1, 0, s)),
        out_shape=out_shape,
        input_output_aliases={0: 0},
        compiler_params=params,
        name="lay_second",
    )(out, swapped)


def solution(mesh):
    heads = mesh.shape["head"]
    fine = Mesh(mesh.devices.reshape(heads, 4, 2, 4, 2), ("head", "z_hi", "z_lo", "y", "core"))
    tok = ("z_hi", "z_lo", "y", "core")
    placed = (
        P(None, tok, "head"),
        P(tok, "head"),
        P(tok, "head"),
        P("head", tok),
        P("head", None, None),
        P("head", None, None),
        P("head", None, None),
    )
    return jax.shard_map(
        local, mesh=fine, in_specs=placed, out_specs=P(None, tok + ("head",), None), check_vma=False
    )
```

```python
import jax
import jax.numpy as jnp
from jax import lax
from jax.experimental import pallas as pl
from jax.experimental.pallas import tpu as pltpu
from jax.sharding import Mesh, PartitionSpec as P

NS_STEPS = 3
coef_first = 3.4445
coef_second = -4.775
coef_third = 2.0315
F32 = jnp.float32
BF16 = jnp.bfloat16
HD = 256
HALF = 128
HEADS_HERE = 5
MATS = 3 * HEADS_HERE
GROUP = 8
N_FAR = 4
VMEM_LIMIT = 48 * 1024 * 1024


def dot_f32(a, b):
    return lax.dot_general(a, b, (((1,), (0,)), ((), ())), preferred_element_type=F32)


def dot_nt(a, b):
    return lax.dot_general(a, b, (((1,), (1,)), ((), ())), preferred_element_type=F32)


def dot_tn(a, b):
    return lax.dot_general(a, b, (((0,), (0,)), ((), ())), preferred_element_type=F32)


def sigmoid(x):
    return 0.5 * jnp.tanh(0.5 * x) + 0.5


def apply_fast(rows, gate, up, down):
    zg = dot_f32(rows, gate)
    zu = dot_f32(rows, up)
    hidden = (zg * sigmoid(zg) * zu).astype(BF16)
    return dot_f32(hidden, down).astype(BF16)


def first_kernel(place_ref, q_ref, g_ref, u_ref, d_ref, *refs):
    out_refs, rows_ref = refs[:-1], refs[-1]
    weights = [ref[0].astype(BF16) for ref in (g_ref, u_ref, d_ref)]
    rows_ref[...] = apply_fast(q_ref[0], *weights)
    count = len(out_refs)
    part = rows_ref.shape[0] // count
    for hop, out_ref in enumerate(out_refs):
        to = lax.rem(place_ref[0] + hop, count)
        out_ref[...] = rows_ref[pl.ds(pl.multiple_of(to * part, part), part), :]


def twist_of(far_ref):
    return jnp.where(far_ref[0] >= N_FAR // 2, 1, 0)


def heads_of(heads, in_refs, scratch):
    k_ref, v_ref, rate_ref, g_ref, u_ref, d_ref = in_refs
    rates, keys, values, gates, ups, downs, rate_sem, sems = scratch
    rate_copy = pltpu.make_async_copy(rate_ref, rates, rate_sem)
    rate_copy.start()
    copies = []
    for at, head in enumerate(heads):
        cols = pl.ds(head * HD, HD)
        pairs = (
            (k_ref.at[:, cols], keys),
            (v_ref.at[:, cols], values),
            (g_ref.at[head], gates),
            (u_ref.at[head], ups),
            (d_ref.at[head], downs),
        )
        copies.append([pltpu.make_async_copy(src, dst.at[at], sems.at[at, i]) for i, (src, dst) in enumerate(pairs)])
        for copy in copies[-1]:
            copy.start()
    rate_copy.wait()
    for at, head in enumerate(heads):
        for copy in copies[at]:
            copy.wait()
        yield (
            head,
            head_grads(
                keys[at],
                values[at],
                rates[head : head + 1, :],
                gates[at].astype(BF16),
                ups[at].astype(BF16),
                downs[at].astype(BF16),
            ),
        )


def sent_kernel(core_ref, far_ref, *refs):
    in_refs, (send_ref, shared_ref), scratch = refs[:6], refs[6:8], refs[8:]
    twist = twist_of(far_ref)

    def run(heads, send_from, keep_from):
        for head, grads in heads_of(heads, in_refs, scratch):
            for mat, grad in enumerate(grads):
                at = head * 3 + mat
                if 0 <= at - send_from < GROUP:
                    send_ref[jnp.bitwise_xor(at - send_from, twist)] = grad
                if 0 <= at - keep_from < 2:
                    shared_ref[at - keep_from] = grad

    @pl.when(core_ref[0] == 0)
    def _():
        run((2, 3, 4), GROUP - 1, 6)

    @pl.when(core_ref[0] != 0)
    def _():
        run((0, 1, 2), 0, GROUP - 1)


def kept_kernel(core_ref, far_ref, *refs):
    in_refs, shared_ref, keep_ref, scratch = refs[:6], refs[6], refs[7], refs[8:]
    twist = twist_of(far_ref)

    def run(heads, keep_from, shared_from):
        for i in range(2):
            keep_ref[jnp.bitwise_xor(shared_from - keep_from + i, twist)] = shared_ref[i]
        for head, grads in heads_of(heads, in_refs, scratch):
            for mat, grad in enumerate(grads):
                keep_ref[jnp.bitwise_xor(head * 3 + mat - keep_from, twist)] = grad

    @pl.when(core_ref[0] == 0)
    def _():
        run((0, 1), 0, 6)

    @pl.when(core_ref[0] != 0)
    def _():
        run((3, 4), GROUP - 1, GROUP - 1)


def head_grads(keys, values, rate, gate, up, down):
    zg = dot_f32(keys, gate)
    zu = dot_f32(keys, up)
    sig = sigmoid(zg)
    silu = zg * sig
    hidden = (silu * zu).astype(BF16)
    rate = jnp.transpose(jnp.broadcast_to(rate, (HALF, rate.shape[1])))
    rate = jnp.concatenate([rate, rate], axis=1)
    dout = (-(rate * values.astype(F32))).astype(BF16)
    dh = dot_nt(dout, down)
    dzu = (dh * silu).astype(BF16)
    dzg = (dh * zu * sig * (1.0 + zg * (1.0 - sig))).astype(BF16)
    pair = dot_tn(keys, jnp.concatenate([dzg, dzu], axis=1)).astype(BF16)
    return pair[:, :HD], pair[:, HD:], dot_tn(hidden, dout).astype(BF16)


def split(x):
    high = x.astype(BF16)
    return high, (x - high.astype(F32)).astype(BF16)


def orth_kernel(*refs):
    out_ref = refs[-1]
    m = refs[0][...].astype(F32)
    for ref in refs[1:-1]:
        m = m + ref[...].astype(F32)
    x = m / (jnp.sqrt(jnp.sum(m * m, keepdims=True)) + 1e-07)
    for sweep in range(NS_STEPS):
        if sweep < NS_STEPS - 1:
            low = x.astype(BF16)
            gram = dot_nt(low, low)
            half = gram.astype(BF16)
            poly = (coef_second * gram + coef_third * dot_f32(half, half)).astype(BF16)
            x = coef_first * x + dot_f32(poly, low)
        else:
            h, l = split(x)
            gram = dot_nt(h, h) + (dot_nt(h, l) + dot_nt(l, h))
            gh, gl = split(gram)
            square = dot_f32(gh, gh) + (dot_f32(gh, gl) + dot_f32(gl, gh))
            ph, pw = split(coef_second * gram + coef_third * square)
            x = coef_first * x + (dot_f32(ph, h) + (dot_f32(ph, l) + dot_f32(pw, h)))
    orth = x.astype(BF16)
    for i in range(out_ref.shape[0]):
        out_ref[i] = orth


def next_weight(fast, orth):
    return (fast - orth.astype(F32)).astype(BF16)


def own_second_kernel(core_ref, far_ref, q_ref, g_ref, u_ref, d_ref, mine_ref, out_ref, *refs):
    g_rest, u_rest, d_rest, u_own, d_own, sems = refs
    twist = twist_of(far_ref)

    def run(own_from, rest_from, base):
        pairs = [(ref.at[pl.ds(own_from, 2)], own) for ref, own in ((u_ref, u_own), (d_ref, d_own))]
        pairs += [(ref.at[pl.ds(rest_from, 3)], rest) for ref, rest in ((g_ref, g_rest), (u_ref, u_rest), (d_ref, d_rest))]
        copies = [pltpu.make_async_copy(src, dst, sems.at[i]) for i, (src, dst) in enumerate(pairs)]
        for copy in copies:
            copy.start()
        for copy in copies[:2]:
            copy.wait()
        for i in range(2):
            head = own_from + i
            fasts = (g_ref[head], u_own[i], d_own[i])
            nexts = [
                next_weight(fast, mine_ref[jnp.bitwise_xor(head * 3 + mat - base, twist)])
                for mat, fast in enumerate(fasts)
            ]
            out_ref[:, i * HD : (i + 1) * HD] = apply_fast(q_ref[0, :, head * HD : (head + 1) * HD], *nexts)
        for copy in copies[2:]:
            copy.wait()

    @pl.when(core_ref[0] == 0)
    def _():
        run(0, 2, 0)

    @pl.when(core_ref[0] != 0)
    def _():
        run(3, 0, GROUP - 1)


def rest_second_kernel(core_ref, far_ref, q_ref, g_rest, u_rest, d_rest, mine_ref, other_ref, own_ref, out_ref):
    twist = twist_of(far_ref)

    def run(own_from, rest_from, base, other_base):
        out_ref[:, own_from * HD : (own_from + 2) * HD] = own_ref[...]
        for i in range(3):
            head = rest_from + i
            nexts = []
            for mat, fast in enumerate((g_rest[i], u_rest[i], d_rest[i])):
                at = head * 3 + mat
                if 0 <= at - base < GROUP:
                    orth = mine_ref[jnp.bitwise_xor(at - base, twist)]
                else:
                    orth = other_ref[jnp.bitwise_xor(at - other_base, twist)]
                nexts.append(next_weight(fast, orth))
            cols = slice(head * HD, (head + 1) * HD)
            out_ref[:, cols] = apply_fast(q_ref[0, :, cols], *nexts)

    @pl.when(core_ref[0] == 0)
    def _():
        run(0, 2, 0, GROUP - 1)

    @pl.when(core_ref[0] != 0)
    def _():
        run(3, 0, GROUP - 1, 0)


def lay_first_kernel(place_ref, *refs):
    hop = pl.program_id(0)
    for i, ref in enumerate(refs[:-1]):

        @pl.when(hop == i)
        def _(ref=ref):
            refs[-1][0] = ref[...]


def lay_second_kernel(buf_ref, rows_ref, out_ref):
    out_ref[...] = rows_ref[...]


def local(queries, key_rows, value_rows, step_rates, gate_fast, up_fast, down_fast):
    rows = key_rows.shape[0]
    width = key_rows.shape[1]
    core = lax.axis_index("core").astype(jnp.int32).reshape(1)
    far = lax.axis_index("z_hi").astype(jnp.int32).reshape(1)
    n_head = lax.axis_size("head")
    part = rows // n_head
    params = pltpu.CompilerParams(dimension_semantics=("arbitrary",), vmem_limit_bytes=VMEM_LIMIT)
    weight_spec = pl.BlockSpec((1, HD, HD), lambda h, *_: (h, 0, 0))
    rows_shape = jax.ShapeDtypeStruct((rows, width), BF16)

    piece_shape = (GROUP, HD, HD)
    piece_spec = pl.BlockSpec(piece_shape, lambda h, *_: (0, 0, 0))
    args = (queries, key_rows, value_rows, step_rates, gate_fast, up_fast, down_fast)
    q_hbm, k_hbm, v_hbm, rate_hbm, g_hbm, u_hbm, d_hbm = [
        pltpu.with_memory_space_constraint(x, pltpu.HBM) for x in args
    ]
    any_spec = pl.BlockSpec(memory_space=pl.ANY)
    piece_array = jax.ShapeDtypeStruct(piece_shape, BF16)
    shared_shape = (2, HD, HD)
    shared_spec = pl.BlockSpec(shared_shape, lambda h, *_: (0, 0, 0))

    def copy_scratch(heads):
        return [
            pltpu.VMEM((HEADS_HERE, rows), F32),
            pltpu.VMEM((heads, rows, HD), BF16),
            pltpu.VMEM((heads, rows, HD), BF16),
            pltpu.VMEM((heads, HD, HD), F32),
            pltpu.VMEM((heads, HD, HD), F32),
            pltpu.VMEM((heads, HD, HD), F32),
            pltpu.SemaphoreType.DMA(()),
            pltpu.SemaphoreType.DMA((heads, 5)),
        ]

    grad_inputs = (k_hbm, v_hbm, rate_hbm, g_hbm, u_hbm, d_hbm)
    send, shared = pl.pallas_call(
        sent_kernel,
        grid_spec=pltpu.PrefetchScalarGridSpec(
            num_scalar_prefetch=2,
            grid=(1,),
            in_specs=[any_spec] * 6,
            out_specs=[piece_spec, shared_spec],
            scratch_shapes=copy_scratch(3),
        ),
        out_shape=[piece_array, jax.ShapeDtypeStruct(shared_shape, BF16)],
        compiler_params=params,
        name="grads_sent",
    )(core, far, *grad_inputs)

    swap = [(0, 1), (1, 0)]
    received = lax.ppermute(send, "core", swap)
    keep = pl.pallas_call(
        kept_kernel,
        grid_spec=pltpu.PrefetchScalarGridSpec(
            num_scalar_prefetch=2,
            grid=(1,),
            in_specs=[any_spec] * 6 + [shared_spec],
            out_specs=piece_spec,
            scratch_shapes=copy_scratch(2),
        ),
        out_shape=piece_array,
        compiler_params=params,
        name="grads_kept",
    )(core, far, *grad_inputs, shared)
    place = lax.axis_index("head").astype(jnp.int32).reshape(1)
    part_spec = pl.BlockSpec((part, HD), lambda h, p: (0, h))
    firsts = pl.pallas_call(
        first_kernel,
        grid_spec=pltpu.PrefetchScalarGridSpec(
            num_scalar_prefetch=1,
            grid=(HEADS_HERE,),
            in_specs=[pl.BlockSpec((1, rows, HD), lambda h, p: (0, 0, h)), weight_spec, weight_spec, weight_spec],
            out_specs=[part_spec] * n_head,
            scratch_shapes=[pltpu.VMEM((rows, HD), BF16)],
        ),
        out_shape=[jax.ShapeDtypeStruct((part, width), BF16)] * n_head,
        compiler_params=params,
        name="first",
    )(place, q_hbm, g_hbm, u_hbm, d_hbm)
    firsts = [firsts[0]] + [
        lax.ppermute(firsts[hop], "head", [(i, (i + hop) % n_head) for i in range(n_head)])
        for hop in range(1, n_head)
    ]

    chip_sum = (keep.astype(F32) + received.astype(F32)).astype(BF16)
    slots = ("y", "z_lo")
    by_slot = lax.all_to_all(chip_sum, slots, split_axis=0, concat_axis=0, tiled=True)
    partial = jnp.sum(by_slot.astype(F32), axis=0).astype(BF16)
    rings = [[2 * i + (slot ^ (i >= N_FAR // 2)) for i in range(N_FAR)] for slot in range(2)]
    partials = [partial] + [
        lax.ppermute(
            partial, ("z_hi", "z_lo"), [(ring[i], ring[(i + hop) % N_FAR]) for ring in rings for i in range(N_FAR)]
        )
        for hop in range(1, N_FAR)
    ]
    late = lax.optimization_barrier((*partials, *firsts))
    partials, firsts = late[:N_FAR], late[N_FAR:]
    orth = pl.pallas_call(
        orth_kernel,
        out_shape=jax.ShapeDtypeStruct(piece_shape, BF16),
        compiler_params=pltpu.CompilerParams(vmem_limit_bytes=VMEM_LIMIT),
        name="orthogonalize",
    )(*partials)
    orth_mine = lax.all_to_all(orth, slots, split_axis=0, concat_axis=0, tiled=True)
    orth_other = lax.ppermute(orth_mine, "core", swap)

    group_spec = pl.BlockSpec((GROUP, HD, HD), lambda i, *_: (0, 0, 0))
    fast_spec = pl.BlockSpec((HEADS_HERE, HD, HD), lambda i, *_: (0, 0, 0))
    query_spec = pl.BlockSpec((1, rows, width), lambda i, *_: (1, 0, 0))
    own_spec = pl.BlockSpec((rows, 2 * HD), lambda i, *_: (0, 0))
    rest_spec = pl.BlockSpec((3, HD, HD), lambda i, *_: (0, 0, 0))
    rest_array = jax.ShapeDtypeStruct((3, HD, HD), F32)
    own, *rest = pl.pallas_call(
        own_second_kernel,
        grid_spec=pltpu.PrefetchScalarGridSpec(
            num_scalar_prefetch=2,
            grid=(1,),
            in_specs=[query_spec, fast_spec, any_spec, any_spec, group_spec],
            out_specs=[own_spec, rest_spec, rest_spec, rest_spec],
            scratch_shapes=[
                pltpu.VMEM((2, HD, HD), F32),
                pltpu.VMEM((2, HD, HD), F32),
                pltpu.SemaphoreType.DMA((5,)),
            ],
        ),
        out_shape=[jax.ShapeDtypeStruct((rows, 2 * HD), BF16), rest_array, rest_array, rest_array],
        compiler_params=params,
        name="second_own",
    )(core, far, queries, gate_fast, u_hbm, d_hbm, orth_mine)
    second = pl.pallas_call(
        rest_second_kernel,
        grid_spec=pltpu.PrefetchScalarGridSpec(
            num_scalar_prefetch=2,
            grid=(1,),
            in_specs=[query_spec, rest_spec, rest_spec, rest_spec, group_spec, group_spec, own_spec],
            out_specs=pl.BlockSpec((rows, width), lambda i, *_: (0, 0)),
        ),
        out_shape=rows_shape,
        compiler_params=params,
        name="second_rest",
    )(core, far, queries, *rest, orth_mine, orth_other, own)

    swapped = lax.all_to_all(second.reshape(n_head, part, width), "head", split_axis=0, concat_axis=0, tiled=True)
    out_shape = jax.ShapeDtypeStruct((2, part, n_head * width), BF16)
    out = pl.pallas_call(
        lay_first_kernel,
        grid_spec=pltpu.PrefetchScalarGridSpec(
            num_scalar_prefetch=1,
            grid=(n_head,),
            in_specs=[pl.BlockSpec((part, width), lambda s, p: (0, 0))] * n_head,
            out_specs=pl.BlockSpec((1, part, width), lambda s, p: (0, 0, lax.rem(p[0] + n_head - s, n_head))),
        ),
        out_shape=out_shape,
        compiler_params=params,
        name="lay_first",
    )(place, *firsts)
    return pl.pallas_call(
        lay_second_kernel,
        grid=(n_head,),
        in_specs=[
            pl.BlockSpec(memory_space=pl.ANY),
            pl.BlockSpec((1, part, width), lambda s: (s, 0, 0)),
        ],
        out_specs=pl.BlockSpec((1, part, width), lambda s: (1, 0, s)),
        out_shape=out_shape,
        input_output_aliases={0: 0},
        compiler_params=params,
        name="lay_second",
    )(out, swapped)


def solution(mesh):
    heads = mesh.shape["head"]
    fine = Mesh(mesh.devices.reshape(heads, 4, 2, 4, 2), ("head", "z_hi", "z_lo", "y", "core"))
    tok = ("z_hi", "z_lo", "y", "core")
    placed = (
        P(None, tok, "head"),
        P(tok, "head"),
        P(tok, "head"),
        P("head", tok),
        P("head", None, None),
        P("head", None, None),
        P("head", None, None),
    )
    return jax.shard_map(
        local, mesh=fine, in_specs=placed, out_specs=P(None, tok + ("head",), None), check_vma=False
    )
```

```python
import jax
import jax.numpy as jnp
from jax import lax
from jax.experimental import pallas as pl
from jax.experimental.pallas import tpu as pltpu
from jax.sharding import Mesh, PartitionSpec as P

NS_STEPS = 3
coef_first = 3.4445
coef_second = -4.775
coef_third = 2.0315
F32 = jnp.float32
BF16 = jnp.bfloat16
HD = 256
HALF = 128
HEADS_HERE = 5
MATS = 3 * HEADS_HERE
GROUP = 8
N_FAR = 4
VMEM_LIMIT = 24 * 1024 * 1024


def dot_f32(a, b):
    return lax.dot_general(a, b, (((1,), (0,)), ((), ())), preferred_element_type=F32)


def dot_nt(a, b):
    return lax.dot_general(a, b, (((1,), (1,)), ((), ())), preferred_element_type=F32)


def dot_tn(a, b):
    return lax.dot_general(a, b, (((0,), (0,)), ((), ())), preferred_element_type=F32)


def sigmoid(x):
    return 0.5 * jnp.tanh(0.5 * x) + 0.5


def apply_fast(rows, gate, up, down):
    zg = dot_f32(rows, gate)
    zu = dot_f32(rows, up)
    hidden = (zg * sigmoid(zg) * zu).astype(BF16)
    return dot_f32(hidden, down).astype(BF16)


def first_kernel(place_ref, q_ref, g_ref, u_ref, d_ref, *refs):
    out_refs, rows_ref = refs[:-1], refs[-1]
    weights = [ref[0].astype(BF16) for ref in (g_ref, u_ref, d_ref)]
    rows_ref[...] = apply_fast(q_ref[0], *weights)
    count = len(out_refs)
    part = rows_ref.shape[0] // count
    for hop, out_ref in enumerate(out_refs):
        to = lax.rem(place_ref[0] + hop, count)
        out_ref[...] = rows_ref[pl.ds(pl.multiple_of(to * part, part), part), :]


def twist_of(far_ref):
    return jnp.where(far_ref[0] >= N_FAR // 2, 1, 0)


def heads_of(heads, in_refs, scratch):
    k_ref, v_ref, rate_ref, g_ref, u_ref, d_ref = in_refs
    rates, keys, values, gates, ups, downs, rate_sem, sems = scratch
    rate_copy = pltpu.make_async_copy(rate_ref, rates, rate_sem)
    rate_copy.start()
    copies = []
    for at, head in enumerate(heads):
        cols = pl.ds(head * HD, HD)
        pairs = (
            (k_ref.at[:, cols], keys),
            (v_ref.at[:, cols], values),
            (g_ref.at[head], gates),
            (u_ref.at[head], ups),
            (d_ref.at[head], downs),
        )
        copies.append([pltpu.make_async_copy(src, dst.at[at], sems.at[at, i]) for i, (src, dst) in enumerate(pairs)])
        for copy in copies[-1]:
            copy.start()
    rate_copy.wait()
    for at, head in enumerate(heads):
        for copy in copies[at]:
            copy.wait()
        yield (
            head,
            head_grads(
                keys[at],
                values[at],
                rates[head : head + 1, :],
                gates[at].astype(BF16),
                ups[at].astype(BF16),
                downs[at].astype(BF16),
            ),
        )


def sent_kernel(core_ref, far_ref, *refs):
    in_refs, (send_ref, shared_ref), scratch = refs[:6], refs[6:8], refs[8:]
    twist = twist_of(far_ref)

    def run(heads, send_from, keep_from):
        for head, grads in heads_of(heads, in_refs, scratch):
            for mat, grad in enumerate(grads):
                at = head * 3 + mat
                if 0 <= at - send_from < GROUP:
                    send_ref[jnp.bitwise_xor(at - send_from, twist)] = grad
                if 0 <= at - keep_from < 2:
                    shared_ref[at - keep_from] = grad

    @pl.when(core_ref[0] == 0)
    def _():
        run((2, 3, 4), GROUP - 1, 6)

    @pl.when(core_ref[0] != 0)
    def _():
        run((0, 1, 2), 0, GROUP - 1)


def kept_kernel(core_ref, far_ref, *refs):
    in_refs, shared_ref, keep_ref, scratch = refs[:6], refs[6], refs[7], refs[8:]
    twist = twist_of(far_ref)

    def run(heads, keep_from, shared_from):
        for i in range(2):
            keep_ref[jnp.bitwise_xor(shared_from - keep_from + i, twist)] = shared_ref[i]
        for head, grads in heads_of(heads, in_refs, scratch):
            for mat, grad in enumerate(grads):
                keep_ref[jnp.bitwise_xor(head * 3 + mat - keep_from, twist)] = grad

    @pl.when(core_ref[0] == 0)
    def _():
        run((0, 1), 0, 6)

    @pl.when(core_ref[0] != 0)
    def _():
        run((3, 4), GROUP - 1, GROUP - 1)


def head_grads(keys, values, rate, gate, up, down):
    zg = dot_f32(keys, gate)
    zu = dot_f32(keys, up)
    sig = sigmoid(zg)
    silu = zg * sig
    hidden = (silu * zu).astype(BF16)
    rate = jnp.transpose(jnp.broadcast_to(rate, (HALF, rate.shape[1])))
    rate = jnp.concatenate([rate, rate], axis=1)
    dout = (-(rate * values.astype(F32))).astype(BF16)
    dh = dot_nt(dout, down)
    dzu = (dh * silu).astype(BF16)
    dzg = (dh * zu * sig * (1.0 + zg * (1.0 - sig))).astype(BF16)
    pair = dot_tn(keys, jnp.concatenate([dzg, dzu], axis=1)).astype(BF16)
    return pair[:, :HD], pair[:, HD:], dot_tn(hidden, dout).astype(BF16)


def split(x):
    high = x.astype(BF16)
    return high, (x - high.astype(F32)).astype(BF16)


def orth_kernel(*refs):
    out_ref = refs[-1]
    m = refs[0][...].astype(F32)
    for ref in refs[1:-1]:
        m = m + ref[...].astype(F32)
    x = m / (jnp.sqrt(jnp.sum(m * m, keepdims=True)) + 1e-07)
    for sweep in range(NS_STEPS):
        if sweep < NS_STEPS - 1:
            low = x.astype(BF16)
            gram = dot_nt(low, low)
            half = gram.astype(BF16)
            poly = (coef_second * gram + coef_third * dot_f32(half, half)).astype(BF16)
            x = coef_first * x + dot_f32(poly, low)
        else:
            h, l = split(x)
            gram = dot_nt(h, h) + (dot_nt(h, l) + dot_nt(l, h))
            gh, gl = split(gram)
            square = dot_f32(gh, gh) + (dot_f32(gh, gl) + dot_f32(gl, gh))
            ph, pw = split(coef_second * gram + coef_third * square)
            x = coef_first * x + (dot_f32(ph, h) + (dot_f32(ph, l) + dot_f32(pw, h)))
    orth = x.astype(BF16)
    for i in range(out_ref.shape[0]):
        out_ref[i] = orth


def next_weight(fast, orth):
    return (fast - orth.astype(F32)).astype(BF16)


def stage_kernel(q_ref, g_ref, u_ref, d_ref, q_out, g_out, u_out, d_out, sems):
    pairs = ((q_ref.at[1], q_out), (g_ref, g_out), (u_ref, u_out), (d_ref, d_out))
    copies = [pltpu.make_async_copy(src, dst, sems.at[i]) for i, (src, dst) in enumerate(pairs)]
    for copy in copies:
        copy.start()
    for copy in copies:
        copy.wait()


def second_head(head, base, twist, q_ref, fast_refs, mine_ref, other_ref=None, other_base=0):
    nexts = []
    for mat, ref in enumerate(fast_refs):
        at = head * 3 + mat
        if 0 <= at - base < GROUP:
            orth = mine_ref[jnp.bitwise_xor(at - base, twist)]
        else:
            orth = other_ref[jnp.bitwise_xor(at - other_base, twist)]
        nexts.append(next_weight(ref[head], orth))
    return apply_fast(q_ref[:, head * HD : (head + 1) * HD], *nexts)


def own_second_kernel(core_ref, far_ref, q_ref, g_ref, u_ref, d_ref, mine_ref, out_ref):
    twist = twist_of(far_ref)

    def run(own_from, base):
        for i in range(2):
            out_ref[:, i * HD : (i + 1) * HD] = second_head(
                own_from + i, base, twist, q_ref, (g_ref, u_ref, d_ref), mine_ref
            )

    @pl.when(core_ref[0] == 0)
    def _():
        run(0, 0)

    @pl.when(core_ref[0] != 0)
    def _():
        run(3, GROUP - 1)


def rest_second_kernel(core_ref, far_ref, q_ref, g_ref, u_ref, d_ref, mine_ref, other_ref, own_ref, out_ref):
    twist = twist_of(far_ref)

    def run(own_from, rest_from, base, other_base):
        out_ref[:, own_from * HD : (own_from + 2) * HD] = own_ref[...]
        for head in range(rest_from, rest_from + 3):
            out_ref[:, head * HD : (head + 1) * HD] = second_head(
                head, base, twist, q_ref, (g_ref, u_ref, d_ref), mine_ref, other_ref, other_base
            )

    @pl.when(core_ref[0] == 0)
    def _():
        run(0, 2, 0, GROUP - 1)

    @pl.when(core_ref[0] != 0)
    def _():
        run(3, 0, GROUP - 1, 0)


def lay_first_kernel(place_ref, *refs):
    hop = pl.program_id(0)
    for i, ref in enumerate(refs[:-1]):

        @pl.when(hop == i)
        def _(ref=ref):
            refs[-1][0] = ref[...]


def lay_second_kernel(buf_ref, rows_ref, out_ref):
    out_ref[...] = rows_ref[...]


def local(queries, key_rows, value_rows, step_rates, gate_fast, up_fast, down_fast):
    rows = key_rows.shape[0]
    width = key_rows.shape[1]
    core = lax.axis_index("core").astype(jnp.int32).reshape(1)
    far = lax.axis_index("z_hi").astype(jnp.int32).reshape(1)
    n_head = lax.axis_size("head")
    part = rows // n_head
    params = pltpu.CompilerParams(dimension_semantics=("arbitrary",), vmem_limit_bytes=VMEM_LIMIT)
    weight_spec = pl.BlockSpec((1, HD, HD), lambda h, *_: (h, 0, 0))
    rows_shape = jax.ShapeDtypeStruct((rows, width), BF16)

    piece_shape = (GROUP, HD, HD)
    piece_spec = pl.BlockSpec(piece_shape, lambda h, *_: (0, 0, 0))
    args = (queries, key_rows, value_rows, step_rates, gate_fast, up_fast, down_fast)
    q_hbm, k_hbm, v_hbm, rate_hbm, g_hbm, u_hbm, d_hbm = [
        pltpu.with_memory_space_constraint(x, pltpu.HBM) for x in args
    ]
    any_spec = pl.BlockSpec(memory_space=pl.ANY)
    piece_array = jax.ShapeDtypeStruct(piece_shape, BF16)
    shared_shape = (2, HD, HD)
    shared_spec = pl.BlockSpec(shared_shape, lambda h, *_: (0, 0, 0))

    def copy_scratch(heads):
        return [
            pltpu.VMEM((HEADS_HERE, rows), F32),
            pltpu.VMEM((heads, rows, HD), BF16),
            pltpu.VMEM((heads, rows, HD), BF16),
            pltpu.VMEM((heads, HD, HD), F32),
            pltpu.VMEM((heads, HD, HD), F32),
            pltpu.VMEM((heads, HD, HD), F32),
            pltpu.SemaphoreType.DMA(()),
            pltpu.SemaphoreType.DMA((heads, 5)),
        ]

    grad_inputs = (k_hbm, v_hbm, rate_hbm, g_hbm, u_hbm, d_hbm)
    send, shared = pl.pallas_call(
        sent_kernel,
        grid_spec=pltpu.PrefetchScalarGridSpec(
            num_scalar_prefetch=2,
            grid=(1,),
            in_specs=[any_spec] * 6,
            out_specs=[piece_spec, shared_spec],
            scratch_shapes=copy_scratch(3),
        ),
        out_shape=[piece_array, jax.ShapeDtypeStruct(shared_shape, BF16)],
        compiler_params=params,
        name="grads_sent",
    )(core, far, *grad_inputs)

    swap = [(0, 1), (1, 0)]
    received = lax.ppermute(send, "core", swap)
    keep = pl.pallas_call(
        kept_kernel,
        grid_spec=pltpu.PrefetchScalarGridSpec(
            num_scalar_prefetch=2,
            grid=(1,),
            in_specs=[any_spec] * 6 + [shared_spec],
            out_specs=piece_spec,
            scratch_shapes=copy_scratch(2),
        ),
        out_shape=piece_array,
        compiler_params=params,
        name="grads_kept",
    )(core, far, *grad_inputs, shared)
    place = lax.axis_index("head").astype(jnp.int32).reshape(1)
    part_spec = pl.BlockSpec((part, HD), lambda h, p: (0, h))
    firsts = pl.pallas_call(
        first_kernel,
        grid_spec=pltpu.PrefetchScalarGridSpec(
            num_scalar_prefetch=1,
            grid=(HEADS_HERE,),
            in_specs=[pl.BlockSpec((1, rows, HD), lambda h, p: (0, 0, h)), weight_spec, weight_spec, weight_spec],
            out_specs=[part_spec] * n_head,
            scratch_shapes=[pltpu.VMEM((rows, HD), BF16)],
        ),
        out_shape=[jax.ShapeDtypeStruct((part, width), BF16)] * n_head,
        compiler_params=params,
        name="first",
    )(place, q_hbm, g_hbm, u_hbm, d_hbm)
    firsts = [firsts[0]] + [
        lax.ppermute(firsts[hop], "head", [(i, (i + hop) % n_head) for i in range(n_head)])
        for hop in range(1, n_head)
    ]

    chip_sum = (keep.astype(F32) + received.astype(F32)).astype(BF16)
    slots = ("y", "z_lo")
    by_slot = lax.all_to_all(chip_sum, slots, split_axis=0, concat_axis=0, tiled=True)
    partial = jnp.sum(by_slot.astype(F32), axis=0).astype(BF16)
    rings = [[2 * i + (slot ^ (i >= N_FAR // 2)) for i in range(N_FAR)] for slot in range(2)]
    partials = [partial] + [
        lax.ppermute(
            partial, ("z_hi", "z_lo"), [(ring[i], ring[(i + hop) % N_FAR]) for ring in rings for i in range(N_FAR)]
        )
        for hop in range(1, N_FAR)
    ]
    rows_full = pl.BlockSpec((rows, width), lambda *_: (0, 0))
    fast_spec = pl.BlockSpec((HEADS_HERE, HD, HD), lambda *_: (0, 0, 0))
    staged = pl.pallas_call(
        stage_kernel,
        grid=(1,),
        in_specs=[any_spec] * 4,
        out_specs=[rows_full] + [fast_spec] * 3,
        out_shape=[rows_shape] + [jax.ShapeDtypeStruct((HEADS_HERE, HD, HD), F32)] * 3,
        scratch_shapes=[pltpu.SemaphoreType.DMA((4,))],
        compiler_params=params,
        name="stage",
    )(q_hbm, g_hbm, u_hbm, d_hbm)
    late = lax.optimization_barrier((*partials, *firsts, *staged))
    partials, firsts, staged = late[:N_FAR], late[N_FAR : N_FAR + n_head], late[N_FAR + n_head :]
    orth = pl.pallas_call(
        orth_kernel,
        out_shape=jax.ShapeDtypeStruct(piece_shape, BF16),
        compiler_params=pltpu.CompilerParams(vmem_limit_bytes=VMEM_LIMIT),
        name="orthogonalize",
    )(*partials)
    orth_mine = lax.all_to_all(orth, slots, split_axis=0, concat_axis=0, tiled=True)
    orth_other = lax.ppermute(orth_mine, "core", swap)

    group_spec = pl.BlockSpec((GROUP, HD, HD), lambda i, *_: (0, 0, 0))
    own_spec = pl.BlockSpec((rows, 2 * HD), lambda *_: (0, 0))
    own = pl.pallas_call(
        own_second_kernel,
        grid_spec=pltpu.PrefetchScalarGridSpec(
            num_scalar_prefetch=2,
            grid=(1,),
            in_specs=[rows_full] + [fast_spec] * 3 + [group_spec],
            out_specs=own_spec,
        ),
        out_shape=jax.ShapeDtypeStruct((rows, 2 * HD), BF16),
        compiler_params=params,
        name="second_own",
    )(core, far, *staged, orth_mine)
    second = pl.pallas_call(
        rest_second_kernel,
        grid_spec=pltpu.PrefetchScalarGridSpec(
            num_scalar_prefetch=2,
            grid=(1,),
            in_specs=[rows_full] + [fast_spec] * 3 + [group_spec] * 2 + [own_spec],
            out_specs=rows_full,
        ),
        out_shape=rows_shape,
        compiler_params=params,
        name="second_rest",
    )(core, far, *staged, orth_mine, orth_other, own)

    swapped = lax.all_to_all(second.reshape(n_head, part, width), "head", split_axis=0, concat_axis=0, tiled=True)
    out_shape = jax.ShapeDtypeStruct((2, part, n_head * width), BF16)
    out = pl.pallas_call(
        lay_first_kernel,
        grid_spec=pltpu.PrefetchScalarGridSpec(
            num_scalar_prefetch=1,
            grid=(n_head,),
            in_specs=[pl.BlockSpec((part, width), lambda s, p: (0, 0))] * n_head,
            out_specs=pl.BlockSpec((1, part, width), lambda s, p: (0, 0, lax.rem(p[0] + n_head - s, n_head))),
        ),
        out_shape=out_shape,
        compiler_params=params,
        name="lay_first",
    )(place, *firsts)
    return pl.pallas_call(
        lay_second_kernel,
        grid=(n_head,),
        in_specs=[
            pl.BlockSpec(memory_space=pl.ANY),
            pl.BlockSpec((1, part, width), lambda s: (s, 0, 0)),
        ],
        out_specs=pl.BlockSpec((1, part, width), lambda s: (1, 0, s)),
        out_shape=out_shape,
        input_output_aliases={0: 0},
        compiler_params=params,
        name="lay_second",
    )(out, swapped)


def solution(mesh):
    heads = mesh.shape["head"]
    fine = Mesh(mesh.devices.reshape(heads, 4, 2, 4, 2), ("head", "z_hi", "z_lo", "y", "core"))
    tok = ("z_hi", "z_lo", "y", "core")
    placed = (
        P(None, tok, "head"),
        P(tok, "head"),
        P(tok, "head"),
        P("head", tok),
        P("head", None, None),
        P("head", None, None),
        P("head", None, None),
    )
    return jax.shard_map(
        local, mesh=fine, in_specs=placed, out_specs=P(None, tok + ("head",), None), check_vma=False
    )
```

```python
import jax
import jax.numpy as jnp
from jax import lax
from jax.experimental import pallas as pl
from jax.experimental.pallas import tpu as pltpu
from jax.sharding import Mesh, PartitionSpec as P

NS_STEPS = 3
coef_first = 3.4445
coef_second = -4.775
coef_third = 2.0315
F32 = jnp.float32
BF16 = jnp.bfloat16
HD = 256
HALF = 128
HEADS_HERE = 5
MATS = 3 * HEADS_HERE
GROUP = 8
N_FAR = 4
VMEM_LIMIT = 24 * 1024 * 1024


def dot_f32(a, b):
    return lax.dot_general(a, b, (((1,), (0,)), ((), ())), preferred_element_type=F32)


def dot_nt(a, b):
    return lax.dot_general(a, b, (((1,), (1,)), ((), ())), preferred_element_type=F32)


def dot_tn(a, b):
    return lax.dot_general(a, b, (((0,), (0,)), ((), ())), preferred_element_type=F32)


def sigmoid(x):
    return 0.5 * jnp.tanh(0.5 * x) + 0.5


def apply_fast(rows, gate, up, down):
    zg = dot_f32(rows, gate)
    zu = dot_f32(rows, up)
    hidden = (zg * sigmoid(zg) * zu).astype(BF16)
    return dot_f32(hidden, down).astype(BF16)


def first_kernel(place_ref, q_ref, g_ref, u_ref, d_ref, *refs):
    out_refs, rows_ref = refs[:-1], refs[-1]
    weights = [ref[0].astype(BF16) for ref in (g_ref, u_ref, d_ref)]
    rows_ref[...] = apply_fast(q_ref[0], *weights)
    count = len(out_refs)
    part = rows_ref.shape[0] // count
    for hop, out_ref in enumerate(out_refs):
        to = lax.rem(place_ref[0] + hop, count)
        out_ref[...] = rows_ref[pl.ds(pl.multiple_of(to * part, part), part), :]


def twist_of(far_ref):
    return jnp.where(far_ref[0] >= N_FAR // 2, 1, 0)


def heads_of(heads, in_refs, scratch):
    k_ref, v_ref, rate_ref, g_ref, u_ref, d_ref = in_refs
    rates, keys, values, gates, ups, downs, rate_sem, sems = scratch
    rate_copy = pltpu.make_async_copy(rate_ref, rates, rate_sem)
    rate_copy.start()
    copies = []
    for at, head in enumerate(heads):
        cols = pl.ds(head * HD, HD)
        pairs = (
            (k_ref.at[:, cols], keys),
            (v_ref.at[:, cols], values),
            (g_ref.at[head], gates),
            (u_ref.at[head], ups),
            (d_ref.at[head], downs),
        )
        copies.append([pltpu.make_async_copy(src, dst.at[at], sems.at[at, i]) for i, (src, dst) in enumerate(pairs)])
        for copy in copies[-1]:
            copy.start()
    rate_copy.wait()
    for at, head in enumerate(heads):
        for copy in copies[at]:
            copy.wait()
        yield (
            head,
            head_grads(
                keys[at],
                values[at],
                rates[head : head + 1, :],
                gates[at].astype(BF16),
                ups[at].astype(BF16),
                downs[at].astype(BF16),
            ),
        )


def sent_kernel(core_ref, far_ref, *refs):
    in_refs, (send_ref, shared_ref), scratch = refs[:6], refs[6:8], refs[8:]
    twist = twist_of(far_ref)

    def run(heads, send_from, keep_from):
        for head, grads in heads_of(heads, in_refs, scratch):
            for mat, grad in enumerate(grads):
                at = head * 3 + mat
                if 0 <= at - send_from < GROUP:
                    send_ref[jnp.bitwise_xor(at - send_from, twist)] = grad
                if 0 <= at - keep_from < 2:
                    shared_ref[at - keep_from] = grad

    @pl.when(core_ref[0] == 0)
    def _():
        run((2, 3, 4), GROUP - 1, 6)

    @pl.when(core_ref[0] != 0)
    def _():
        run((0, 1, 2), 0, GROUP - 1)


def kept_kernel(core_ref, far_ref, *refs):
    in_refs, shared_ref, keep_ref, scratch = refs[:6], refs[6], refs[7], refs[8:]
    twist = twist_of(far_ref)

    def run(heads, keep_from, shared_from):
        for i in range(2):
            keep_ref[jnp.bitwise_xor(shared_from - keep_from + i, twist)] = shared_ref[i]
        for head, grads in heads_of(heads, in_refs, scratch):
            for mat, grad in enumerate(grads):
                keep_ref[jnp.bitwise_xor(head * 3 + mat - keep_from, twist)] = grad

    @pl.when(core_ref[0] == 0)
    def _():
        run((0, 1), 0, 6)

    @pl.when(core_ref[0] != 0)
    def _():
        run((3, 4), GROUP - 1, GROUP - 1)


def head_grads(keys, values, rate, gate, up, down):
    zg = dot_f32(keys, gate)
    zu = dot_f32(keys, up)
    sig = sigmoid(zg)
    silu = zg * sig
    hidden = (silu * zu).astype(BF16)
    rate = jnp.transpose(jnp.broadcast_to(rate, (HALF, rate.shape[1])))
    rate = jnp.concatenate([rate, rate], axis=1)
    dout = (-(rate * values.astype(F32))).astype(BF16)
    dh = dot_nt(dout, down)
    dzu = (dh * silu).astype(BF16)
    dzg = (dh * zu * sig * (1.0 + zg * (1.0 - sig))).astype(BF16)
    pair = dot_tn(keys, jnp.concatenate([dzg, dzu], axis=1)).astype(BF16)
    return pair[:, :HD], pair[:, HD:], dot_tn(hidden, dout).astype(BF16)


def split(x):
    high = x.astype(BF16)
    return high, (x - high.astype(F32)).astype(BF16)


def orth_kernel(*refs):
    out_ref = refs[-1]
    m = refs[0][...].astype(F32)
    for ref in refs[1:-1]:
        m = m + ref[...].astype(F32)
    x = m / (jnp.sqrt(jnp.sum(m * m, keepdims=True)) + 1e-07)
    for sweep in range(NS_STEPS):
        if sweep < NS_STEPS - 1:
            low = x.astype(BF16)
            gram = dot_nt(low, low)
            half = gram.astype(BF16)
            poly = (coef_second * gram + coef_third * dot_f32(half, half)).astype(BF16)
            x = coef_first * x + dot_f32(poly, low)
        else:
            h, l = split(x)
            gram = dot_nt(h, h) + (dot_nt(h, l) + dot_nt(l, h))
            gh, gl = split(gram)
            square = dot_f32(gh, gh) + (dot_f32(gh, gl) + dot_f32(gl, gh))
            ph, pw = split(coef_second * gram + coef_third * square)
            x = coef_first * x + (dot_f32(ph, h) + (dot_f32(ph, l) + dot_f32(pw, h)))
    orth = x.astype(BF16)
    for i in range(out_ref.shape[0]):
        out_ref[i] = orth


def next_weight(fast, orth):
    return (fast - orth.astype(F32)).astype(BF16)


def stage_kernel(q_ref, g_ref, u_ref, d_ref, q_out, g_out, u_out, d_out, sems):
    pairs = ((q_ref.at[1], q_out), (g_ref, g_out), (u_ref, u_out), (d_ref, d_out))
    copies = [pltpu.make_async_copy(src, dst, sems.at[i]) for i, (src, dst) in enumerate(pairs)]
    for copy in copies:
        copy.start()
    for copy in copies:
        copy.wait()


def second_head(head, base, twist, q_ref, fast_refs, mine_ref, other_ref=None, other_base=0):
    nexts = []
    for mat, ref in enumerate(fast_refs):
        at = head * 3 + mat
        if 0 <= at - base < GROUP:
            orth = mine_ref[jnp.bitwise_xor(at - base, twist)]
        else:
            orth = other_ref[jnp.bitwise_xor(at - other_base, twist)]
        nexts.append(next_weight(ref[head], orth))
    return apply_fast(q_ref[:, head * HD : (head + 1) * HD], *nexts)


def own_second_kernel(core_ref, far_ref, q_ref, g_ref, u_ref, d_ref, mine_ref, out_ref):
    twist = twist_of(far_ref)

    def run(own_from, base):
        for i in range(2):
            out_ref[:, i * HD : (i + 1) * HD] = second_head(
                own_from + i, base, twist, q_ref, (g_ref, u_ref, d_ref), mine_ref
            )

    @pl.when(core_ref[0] == 0)
    def _():
        run(0, 0)

    @pl.when(core_ref[0] != 0)
    def _():
        run(3, GROUP - 1)


def rest_second_kernel(core_ref, far_ref, q_ref, g_ref, u_ref, d_ref, mine_ref, other_ref, own_ref, out_ref):
    twist = twist_of(far_ref)

    def run(own_from, rest_from, base, other_base):
        out_ref[:, own_from * HD : (own_from + 2) * HD] = own_ref[...]
        for head in range(rest_from, rest_from + 3):
            out_ref[:, head * HD : (head + 1) * HD] = second_head(
                head, base, twist, q_ref, (g_ref, u_ref, d_ref), mine_ref, other_ref, other_base
            )

    @pl.when(core_ref[0] == 0)
    def _():
        run(0, 2, 0, GROUP - 1)

    @pl.when(core_ref[0] != 0)
    def _():
        run(3, 0, GROUP - 1, 0)


def lay_first_kernel(place_ref, *refs):
    hop = pl.program_id(0)
    for i, ref in enumerate(refs[:-1]):

        @pl.when(hop == i)
        def _(ref=ref):
            refs[-1][0] = ref[...]


def lay_second_kernel(buf_ref, rows_ref, out_ref, sems):
    count, _, width = rows_ref.shape
    copies = [
        pltpu.make_async_copy(rows_ref.at[i], out_ref.at[1, :, pl.ds(i * width, width)], sems.at[i])
        for i in range(count)
    ]
    for copy in copies:
        copy.start()
    for copy in copies:
        copy.wait()


def local(queries, key_rows, value_rows, step_rates, gate_fast, up_fast, down_fast):
    rows = key_rows.shape[0]
    width = key_rows.shape[1]
    core = lax.axis_index("core").astype(jnp.int32).reshape(1)
    far = lax.axis_index("z_hi").astype(jnp.int32).reshape(1)
    n_head = lax.axis_size("head")
    part = rows // n_head
    params = pltpu.CompilerParams(dimension_semantics=("arbitrary",), vmem_limit_bytes=VMEM_LIMIT)
    weight_spec = pl.BlockSpec((1, HD, HD), lambda h, *_: (h, 0, 0))
    rows_shape = jax.ShapeDtypeStruct((rows, width), BF16)

    piece_shape = (GROUP, HD, HD)
    piece_spec = pl.BlockSpec(piece_shape, lambda h, *_: (0, 0, 0))
    args = (queries, key_rows, value_rows, step_rates, gate_fast, up_fast, down_fast)
    q_hbm, k_hbm, v_hbm, rate_hbm, g_hbm, u_hbm, d_hbm = [
        pltpu.with_memory_space_constraint(x, pltpu.HBM) for x in args
    ]
    any_spec = pl.BlockSpec(memory_space=pl.ANY)
    piece_array = jax.ShapeDtypeStruct(piece_shape, BF16)
    shared_shape = (2, HD, HD)
    shared_spec = pl.BlockSpec(shared_shape, lambda h, *_: (0, 0, 0))

    def copy_scratch(heads):
        return [
            pltpu.VMEM((HEADS_HERE, rows), F32),
            pltpu.VMEM((heads, rows, HD), BF16),
            pltpu.VMEM((heads, rows, HD), BF16),
            pltpu.VMEM((heads, HD, HD), F32),
            pltpu.VMEM((heads, HD, HD), F32),
            pltpu.VMEM((heads, HD, HD), F32),
            pltpu.SemaphoreType.DMA(()),
            pltpu.SemaphoreType.DMA((heads, 5)),
        ]

    grad_inputs = (k_hbm, v_hbm, rate_hbm, g_hbm, u_hbm, d_hbm)
    send, shared = pl.pallas_call(
        sent_kernel,
        grid_spec=pltpu.PrefetchScalarGridSpec(
            num_scalar_prefetch=2,
            grid=(1,),
            in_specs=[any_spec] * 6,
            out_specs=[piece_spec, shared_spec],
            scratch_shapes=copy_scratch(3),
        ),
        out_shape=[piece_array, jax.ShapeDtypeStruct(shared_shape, BF16)],
        compiler_params=params,
        name="grads_sent",
    )(core, far, *grad_inputs)

    swap = [(0, 1), (1, 0)]
    received = lax.ppermute(send, "core", swap)
    keep = pl.pallas_call(
        kept_kernel,
        grid_spec=pltpu.PrefetchScalarGridSpec(
            num_scalar_prefetch=2,
            grid=(1,),
            in_specs=[any_spec] * 6 + [shared_spec],
            out_specs=piece_spec,
            scratch_shapes=copy_scratch(2),
        ),
        out_shape=piece_array,
        compiler_params=params,
        name="grads_kept",
    )(core, far, *grad_inputs, shared)
    place = lax.axis_index("head").astype(jnp.int32).reshape(1)
    part_spec = pl.BlockSpec((part, HD), lambda h, p: (0, h))
    firsts = pl.pallas_call(
        first_kernel,
        grid_spec=pltpu.PrefetchScalarGridSpec(
            num_scalar_prefetch=1,
            grid=(HEADS_HERE,),
            in_specs=[pl.BlockSpec((1, rows, HD), lambda h, p: (0, 0, h)), weight_spec, weight_spec, weight_spec],
            out_specs=[part_spec] * n_head,
            scratch_shapes=[pltpu.VMEM((rows, HD), BF16)],
        ),
        out_shape=[jax.ShapeDtypeStruct((part, width), BF16)] * n_head,
        compiler_params=params,
        name="first",
    )(place, q_hbm, g_hbm, u_hbm, d_hbm)
    firsts = [firsts[0]] + [
        lax.ppermute(firsts[hop], "head", [(i, (i + hop) % n_head) for i in range(n_head)])
        for hop in range(1, n_head)
    ]

    chip_sum = (keep.astype(F32) + received.astype(F32)).astype(BF16)
    slots = ("y", "z_lo")
    by_slot = lax.all_to_all(chip_sum, slots, split_axis=0, concat_axis=0, tiled=True)
    partial = jnp.sum(by_slot.astype(F32), axis=0).astype(BF16)
    rings = [[2 * i + (slot ^ (i >= N_FAR // 2)) for i in range(N_FAR)] for slot in range(2)]
    partials = [partial] + [
        lax.ppermute(
            partial, ("z_hi", "z_lo"), [(ring[i], ring[(i + hop) % N_FAR]) for ring in rings for i in range(N_FAR)]
        )
        for hop in (2, 1, 3)
    ]
    rows_full = pl.BlockSpec((rows, width), lambda *_: (0, 0))
    fast_spec = pl.BlockSpec((HEADS_HERE, HD, HD), lambda *_: (0, 0, 0))
    staged = pl.pallas_call(
        stage_kernel,
        grid=(1,),
        in_specs=[any_spec] * 4,
        out_specs=[rows_full] + [fast_spec] * 3,
        out_shape=[rows_shape] + [jax.ShapeDtypeStruct((HEADS_HERE, HD, HD), F32)] * 3,
        scratch_shapes=[pltpu.SemaphoreType.DMA((4,))],
        compiler_params=params,
        name="stage",
    )(q_hbm, g_hbm, u_hbm, d_hbm)
    late = lax.optimization_barrier((*partials, *firsts, *staged))
    partials, firsts, staged = late[:N_FAR], late[N_FAR : N_FAR + n_head], late[N_FAR + n_head :]
    orth = pl.pallas_call(
        orth_kernel,
        out_shape=jax.ShapeDtypeStruct(piece_shape, BF16),
        compiler_params=pltpu.CompilerParams(vmem_limit_bytes=VMEM_LIMIT),
        name="orthogonalize",
    )(*partials)
    orth_mine = lax.all_to_all(orth, slots, split_axis=0, concat_axis=0, tiled=True)
    orth_other = lax.ppermute(orth_mine, "core", swap)

    group_spec = pl.BlockSpec((GROUP, HD, HD), lambda i, *_: (0, 0, 0))
    own_spec = pl.BlockSpec((rows, 2 * HD), lambda *_: (0, 0))
    own = pl.pallas_call(
        own_second_kernel,
        grid_spec=pltpu.PrefetchScalarGridSpec(
            num_scalar_prefetch=2,
            grid=(1,),
            in_specs=[rows_full] + [fast_spec] * 3 + [group_spec],
            out_specs=own_spec,
        ),
        out_shape=jax.ShapeDtypeStruct((rows, 2 * HD), BF16),
        compiler_params=params,
        name="second_own",
    )(core, far, *staged, orth_mine)
    second = pl.pallas_call(
        rest_second_kernel,
        grid_spec=pltpu.PrefetchScalarGridSpec(
            num_scalar_prefetch=2,
            grid=(1,),
            in_specs=[rows_full] + [fast_spec] * 3 + [group_spec] * 2 + [own_spec],
            out_specs=rows_full,
        ),
        out_shape=rows_shape,
        compiler_params=params,
        name="second_rest",
    )(core, far, *staged, orth_mine, orth_other, own)

    swapped = lax.all_to_all(second.reshape(n_head, part, width), "head", split_axis=0, concat_axis=0, tiled=True)
    out_shape = jax.ShapeDtypeStruct((2, part, n_head * width), BF16)
    out = pl.pallas_call(
        lay_first_kernel,
        grid_spec=pltpu.PrefetchScalarGridSpec(
            num_scalar_prefetch=1,
            grid=(n_head,),
            in_specs=[pl.BlockSpec((part, width), lambda s, p: (0, 0))] * n_head,
            out_specs=pl.BlockSpec((1, part, width), lambda s, p: (0, 0, lax.rem(p[0] + n_head - s, n_head))),
        ),
        out_shape=out_shape,
        compiler_params=params,
        name="lay_first",
    )(place, *firsts)
    return pl.pallas_call(
        lay_second_kernel,
        grid=(1,),
        in_specs=[any_spec, pl.BlockSpec((n_head, part, width), lambda s: (0, 0, 0))],
        out_specs=any_spec,
        out_shape=out_shape,
        input_output_aliases={0: 0},
        scratch_shapes=[pltpu.SemaphoreType.DMA((n_head,))],
        compiler_params=params,
        name="lay_second",
    )(out, swapped)


def solution(mesh):
    heads = mesh.shape["head"]
    fine = Mesh(mesh.devices.reshape(heads, 4, 2, 4, 2), ("head", "z_hi", "z_lo", "y", "core"))
    tok = ("z_hi", "z_lo", "y", "core")
    placed = (
        P(None, tok, "head"),
        P(tok, "head"),
        P(tok, "head"),
        P("head", tok),
        P("head", None, None),
        P("head", None, None),
        P("head", None, None),
    )
    return jax.shard_map(
        local, mesh=fine, in_specs=placed, out_specs=P(None, tok + ("head",), None), check_vma=False
    )
```

```python
import jax
import jax.numpy as jnp
from jax import lax
from jax.experimental import pallas as pl
from jax.experimental.pallas import tpu as pltpu
from jax.sharding import Mesh, PartitionSpec as P

NS_STEPS = 3
coef_first = 3.4445
coef_second = -4.775
coef_third = 2.0315
F32 = jnp.float32
BF16 = jnp.bfloat16
HD = 256
HALF = 128
HEADS_HERE = 5
MATS = 3 * HEADS_HERE
GROUP = 8
N_FAR = 4
VMEM_LIMIT = 24 * 1024 * 1024


def dot_f32(a, b):
    return lax.dot_general(a, b, (((1,), (0,)), ((), ())), preferred_element_type=F32)


def dot_nt(a, b):
    return lax.dot_general(a, b, (((1,), (1,)), ((), ())), preferred_element_type=F32)


def dot_tn(a, b):
    return lax.dot_general(a, b, (((0,), (0,)), ((), ())), preferred_element_type=F32)


def sigmoid(x):
    return 0.5 * jnp.tanh(0.5 * x) + 0.5


def apply_fast(rows, gate, up, down):
    zg = dot_f32(rows, gate)
    zu = dot_f32(rows, up)
    hidden = (zg * sigmoid(zg) * zu).astype(BF16)
    return dot_f32(hidden, down).astype(BF16)


def first_kernel(place_ref, q_ref, g_ref, u_ref, d_ref, *refs):
    out_refs, rows_ref = refs[:-1], refs[-1]
    weights = [ref[0].astype(BF16) for ref in (g_ref, u_ref, d_ref)]
    rows_ref[...] = apply_fast(q_ref[0], *weights)
    count = len(out_refs)
    part = rows_ref.shape[0] // count
    for hop, out_ref in enumerate(out_refs):
        to = lax.rem(place_ref[0] + hop, count)
        out_ref[...] = rows_ref[pl.ds(pl.multiple_of(to * part, part), part), :]


def twist_of(far_ref):
    return jnp.where(far_ref[0] >= N_FAR // 2, 1, 0)


def heads_of(heads, in_refs, scratch):
    k_ref, v_ref, rate_ref, g_ref, u_ref, d_ref = in_refs
    rates, keys, values, gates, ups, downs, rate_sem, sems = scratch
    rate_copy = pltpu.make_async_copy(rate_ref, rates, rate_sem)
    rate_copy.start()
    cols = pl.ds(heads[0] * HD, len(heads) * HD)
    wide = [
        pltpu.make_async_copy(k_ref.at[:, cols], keys, sems.at[0, 3]),
        pltpu.make_async_copy(v_ref.at[:, cols], values, sems.at[0, 4]),
    ]
    for copy in wide:
        copy.start()
    copies = []
    for at, head in enumerate(heads):
        pairs = ((g_ref, gates), (u_ref, ups), (d_ref, downs))
        copies.append(
            [pltpu.make_async_copy(src.at[head], dst.at[at], sems.at[at, i]) for i, (src, dst) in enumerate(pairs)]
        )
        for copy in copies[-1]:
            copy.start()
    rate_copy.wait()
    for copy in wide:
        copy.wait()
    for at, head in enumerate(heads):
        for copy in copies[at]:
            copy.wait()
        mine = slice(at * HD, (at + 1) * HD)
        yield (
            head,
            head_grads(
                keys[:, mine],
                values[:, mine],
                rates[head : head + 1, :],
                gates[at].astype(BF16),
                ups[at].astype(BF16),
                downs[at].astype(BF16),
            ),
        )


def sent_kernel(core_ref, far_ref, *refs):
    in_refs, (send_ref, shared_ref), scratch = refs[:6], refs[6:8], refs[8:]
    twist = twist_of(far_ref)

    def run(heads, send_from, keep_from):
        for head, grads in heads_of(heads, in_refs, scratch):
            for mat, grad in enumerate(grads):
                at = head * 3 + mat
                if 0 <= at - send_from < GROUP:
                    send_ref[jnp.bitwise_xor(at - send_from, twist)] = grad
                if 0 <= at - keep_from < 2:
                    shared_ref[at - keep_from] = grad

    @pl.when(core_ref[0] == 0)
    def _():
        run((2, 3, 4), GROUP - 1, 6)

    @pl.when(core_ref[0] != 0)
    def _():
        run((0, 1, 2), 0, GROUP - 1)


def kept_kernel(core_ref, far_ref, *refs):
    in_refs, shared_ref, keep_ref, scratch = refs[:6], refs[6], refs[7], refs[8:]
    twist = twist_of(far_ref)

    def run(heads, keep_from, shared_from):
        for i in range(2):
            keep_ref[jnp.bitwise_xor(shared_from - keep_from + i, twist)] = shared_ref[i]
        for head, grads in heads_of(heads, in_refs, scratch):
            for mat, grad in enumerate(grads):
                keep_ref[jnp.bitwise_xor(head * 3 + mat - keep_from, twist)] = grad

    @pl.when(core_ref[0] == 0)
    def _():
        run((0, 1), 0, 6)

    @pl.when(core_ref[0] != 0)
    def _():
        run((3, 4), GROUP - 1, GROUP - 1)


def head_grads(keys, values, rate, gate, up, down):
    zg = dot_f32(keys, gate)
    zu = dot_f32(keys, up)
    sig = sigmoid(zg)
    silu = zg * sig
    hidden = (silu * zu).astype(BF16)
    rate = jnp.transpose(jnp.broadcast_to(rate, (HALF, rate.shape[1])))
    rate = jnp.concatenate([rate, rate], axis=1)
    dout = (-(rate * values.astype(F32))).astype(BF16)
    dh = dot_nt(dout, down)
    dzu = (dh * silu).astype(BF16)
    dzg = (dh * zu * sig * (1.0 + zg * (1.0 - sig))).astype(BF16)
    pair = dot_tn(keys, jnp.concatenate([dzg, dzu], axis=1)).astype(BF16)
    return pair[:, :HD], pair[:, HD:], dot_tn(hidden, dout).astype(BF16)


def split(x):
    high = x.astype(BF16)
    return high, (x - high.astype(F32)).astype(BF16)


def orth_kernel(*refs):
    out_ref = refs[-1]
    m = refs[0][...].astype(F32)
    for ref in refs[1:-1]:
        m = m + ref[...].astype(F32)
    x = m / (jnp.sqrt(jnp.sum(m * m, keepdims=True)) + 1e-07)
    for sweep in range(NS_STEPS):
        if sweep < NS_STEPS - 1:
            low = x.astype(BF16)
            gram = dot_nt(low, low)
            half = gram.astype(BF16)
            poly = (coef_second * gram + coef_third * dot_f32(half, half)).astype(BF16)
            x = coef_first * x + dot_f32(poly, low)
        else:
            h, l = split(x)
            gram = dot_nt(h, h) + (dot_nt(h, l) + dot_nt(l, h))
            gh, gl = split(gram)
            square = dot_f32(gh, gh) + (dot_f32(gh, gl) + dot_f32(gl, gh))
            ph, pw = split(coef_second * gram + coef_third * square)
            x = coef_first * x + (dot_f32(ph, h) + (dot_f32(ph, l) + dot_f32(pw, h)))
    orth = x.astype(BF16)
    for i in range(out_ref.shape[0]):
        out_ref[i] = orth


def next_weight(fast, orth):
    return (fast - orth.astype(F32)).astype(BF16)


def stage_kernel(q_ref, g_ref, u_ref, d_ref, q_out, g_out, u_out, d_out, sems):
    pairs = ((q_ref.at[1], q_out), (g_ref, g_out), (u_ref, u_out), (d_ref, d_out))
    copies = [pltpu.make_async_copy(src, dst, sems.at[i]) for i, (src, dst) in enumerate(pairs)]
    for copy in copies:
        copy.start()
    for copy in copies:
        copy.wait()


def second_head(head, base, twist, q_ref, fast_refs, mine_ref, other_ref=None, other_base=0):
    nexts = []
    for mat, ref in enumerate(fast_refs):
        at = head * 3 + mat
        if 0 <= at - base < GROUP:
            orth = mine_ref[jnp.bitwise_xor(at - base, twist)]
        else:
            orth = other_ref[jnp.bitwise_xor(at - other_base, twist)]
        nexts.append(next_weight(ref[head], orth))
    return apply_fast(q_ref[:, head * HD : (head + 1) * HD], *nexts)


def own_second_kernel(core_ref, far_ref, q_ref, g_ref, u_ref, d_ref, mine_ref, out_ref):
    twist = twist_of(far_ref)

    def run(own_from, base):
        for i in range(2):
            out_ref[:, i * HD : (i + 1) * HD] = second_head(
                own_from + i, base, twist, q_ref, (g_ref, u_ref, d_ref), mine_ref
            )

    @pl.when(core_ref[0] == 0)
    def _():
        run(0, 0)

    @pl.when(core_ref[0] != 0)
    def _():
        run(3, GROUP - 1)


def rest_second_kernel(core_ref, far_ref, q_ref, g_ref, u_ref, d_ref, mine_ref, other_ref, own_ref, out_ref):
    twist = twist_of(far_ref)

    def run(own_from, rest_from, base, other_base):
        out_ref[:, own_from * HD : (own_from + 2) * HD] = own_ref[...]
        for head in range(rest_from, rest_from + 3):
            out_ref[:, head * HD : (head + 1) * HD] = second_head(
                head, base, twist, q_ref, (g_ref, u_ref, d_ref), mine_ref, other_ref, other_base
            )

    @pl.when(core_ref[0] == 0)
    def _():
        run(0, 2, 0, GROUP - 1)

    @pl.when(core_ref[0] != 0)
    def _():
        run(3, 0, GROUP - 1, 0)


def lay_first_kernel(place_ref, *refs):
    hop = pl.program_id(0)
    for i, ref in enumerate(refs[:-1]):

        @pl.when(hop == i)
        def _(ref=ref):
            refs[-1][0] = ref[...]


def lay_second_kernel(buf_ref, rows_ref, out_ref, sems):
    count, _, width = rows_ref.shape
    copies = [
        pltpu.make_async_copy(rows_ref.at[i], out_ref.at[1, :, pl.ds(i * width, width)], sems.at[i])
        for i in range(count)
    ]
    for copy in copies:
        copy.start()
    for copy in copies:
        copy.wait()


def local(queries, key_rows, value_rows, step_rates, gate_fast, up_fast, down_fast):
    rows = key_rows.shape[0]
    width = key_rows.shape[1]
    core = lax.axis_index("core").astype(jnp.int32).reshape(1)
    far = lax.axis_index("z_hi").astype(jnp.int32).reshape(1)
    n_head = lax.axis_size("head")
    part = rows // n_head
    params = pltpu.CompilerParams(dimension_semantics=("arbitrary",), vmem_limit_bytes=VMEM_LIMIT)
    weight_spec = pl.BlockSpec((1, HD, HD), lambda h, *_: (h, 0, 0))
    rows_shape = jax.ShapeDtypeStruct((rows, width), BF16)

    piece_shape = (GROUP, HD, HD)
    piece_spec = pl.BlockSpec(piece_shape, lambda h, *_: (0, 0, 0))
    args = (queries, key_rows, value_rows, step_rates, gate_fast, up_fast, down_fast)
    q_hbm, k_hbm, v_hbm, rate_hbm, g_hbm, u_hbm, d_hbm = [
        pltpu.with_memory_space_constraint(x, pltpu.HBM) for x in args
    ]
    any_spec = pl.BlockSpec(memory_space=pl.ANY)
    piece_array = jax.ShapeDtypeStruct(piece_shape, BF16)
    shared_shape = (2, HD, HD)
    shared_spec = pl.BlockSpec(shared_shape, lambda h, *_: (0, 0, 0))

    def copy_scratch(heads):
        return [
            pltpu.VMEM((HEADS_HERE, rows), F32),
            pltpu.VMEM((rows, heads * HD), BF16),
            pltpu.VMEM((rows, heads * HD), BF16),
            pltpu.VMEM((heads, HD, HD), F32),
            pltpu.VMEM((heads, HD, HD), F32),
            pltpu.VMEM((heads, HD, HD), F32),
            pltpu.SemaphoreType.DMA(()),
            pltpu.SemaphoreType.DMA((heads, 5)),
        ]

    grad_inputs = (k_hbm, v_hbm, rate_hbm, g_hbm, u_hbm, d_hbm)
    send, shared = pl.pallas_call(
        sent_kernel,
        grid_spec=pltpu.PrefetchScalarGridSpec(
            num_scalar_prefetch=2,
            grid=(1,),
            in_specs=[any_spec] * 6,
            out_specs=[piece_spec, shared_spec],
            scratch_shapes=copy_scratch(3),
        ),
        out_shape=[piece_array, jax.ShapeDtypeStruct(shared_shape, BF16)],
        compiler_params=params,
        name="grads_sent",
    )(core, far, *grad_inputs)

    swap = [(0, 1), (1, 0)]
    received = lax.ppermute(send, "core", swap)
    keep = pl.pallas_call(
        kept_kernel,
        grid_spec=pltpu.PrefetchScalarGridSpec(
            num_scalar_prefetch=2,
            grid=(1,),
            in_specs=[any_spec] * 6 + [shared_spec],
            out_specs=piece_spec,
            scratch_shapes=copy_scratch(2),
        ),
        out_shape=piece_array,
        compiler_params=params,
        name="grads_kept",
    )(core, far, *grad_inputs, shared)
    place = lax.axis_index("head").astype(jnp.int32).reshape(1)
    part_spec = pl.BlockSpec((part, HD), lambda h, p: (0, h))
    firsts = pl.pallas_call(
        first_kernel,
        grid_spec=pltpu.PrefetchScalarGridSpec(
            num_scalar_prefetch=1,
            grid=(HEADS_HERE,),
            in_specs=[pl.BlockSpec((1, rows, HD), lambda h, p: (0, 0, h)), weight_spec, weight_spec, weight_spec],
            out_specs=[part_spec] * n_head,
            scratch_shapes=[pltpu.VMEM((rows, HD), BF16)],
        ),
        out_shape=[jax.ShapeDtypeStruct((part, width), BF16)] * n_head,
        compiler_params=params,
        name="first",
    )(place, q_hbm, g_hbm, u_hbm, d_hbm)
    firsts = [firsts[0]] + [
        lax.ppermute(firsts[hop], "head", [(i, (i + hop) % n_head) for i in range(n_head)])
        for hop in range(1, n_head)
    ]

    chip_sum = (keep.astype(F32) + received.astype(F32)).astype(BF16)
    slots = ("y", "z_lo")
    by_slot = lax.all_to_all(chip_sum, slots, split_axis=0, concat_axis=0, tiled=True)
    partial = jnp.sum(by_slot.astype(F32), axis=0).astype(BF16)
    rings = [[2 * i + (slot ^ (i >= N_FAR // 2)) for i in range(N_FAR)] for slot in range(2)]
    partials = [partial] + [
        lax.ppermute(
            partial, ("z_hi", "z_lo"), [(ring[i], ring[(i + hop) % N_FAR]) for ring in rings for i in range(N_FAR)]
        )
        for hop in (2, 1, 3)
    ]
    rows_full = pl.BlockSpec((rows, width), lambda *_: (0, 0))
    fast_spec = pl.BlockSpec((HEADS_HERE, HD, HD), lambda *_: (0, 0, 0))
    staged = pl.pallas_call(
        stage_kernel,
        grid=(1,),
        in_specs=[any_spec] * 4,
        out_specs=[rows_full] + [fast_spec] * 3,
        out_shape=[rows_shape] + [jax.ShapeDtypeStruct((HEADS_HERE, HD, HD), F32)] * 3,
        scratch_shapes=[pltpu.SemaphoreType.DMA((4,))],
        compiler_params=params,
        name="stage",
    )(q_hbm, g_hbm, u_hbm, d_hbm)
    late = lax.optimization_barrier((*partials, *firsts, *staged))
    partials, firsts, staged = late[:N_FAR], late[N_FAR : N_FAR + n_head], late[N_FAR + n_head :]
    orth = pl.pallas_call(
        orth_kernel,
        out_shape=jax.ShapeDtypeStruct(piece_shape, BF16),
        compiler_params=pltpu.CompilerParams(vmem_limit_bytes=VMEM_LIMIT),
        name="orthogonalize",
    )(*partials)
    orth_mine = lax.all_to_all(orth, slots, split_axis=0, concat_axis=0, tiled=True)
    orth_other = lax.ppermute(orth_mine, "core", swap)

    group_spec = pl.BlockSpec((GROUP, HD, HD), lambda i, *_: (0, 0, 0))
    own_spec = pl.BlockSpec((rows, 2 * HD), lambda *_: (0, 0))
    own = pl.pallas_call(
        own_second_kernel,
        grid_spec=pltpu.PrefetchScalarGridSpec(
            num_scalar_prefetch=2,
            grid=(1,),
            in_specs=[rows_full] + [fast_spec] * 3 + [group_spec],
            out_specs=own_spec,
        ),
        out_shape=jax.ShapeDtypeStruct((rows, 2 * HD), BF16),
        compiler_params=params,
        name="second_own",
    )(core, far, *staged, orth_mine)
    second = pl.pallas_call(
        rest_second_kernel,
        grid_spec=pltpu.PrefetchScalarGridSpec(
            num_scalar_prefetch=2,
            grid=(1,),
            in_specs=[rows_full] + [fast_spec] * 3 + [group_spec] * 2 + [own_spec],
            out_specs=rows_full,
        ),
        out_shape=rows_shape,
        compiler_params=params,
        name="second_rest",
    )(core, far, *staged, orth_mine, orth_other, own)

    swapped = lax.all_to_all(second.reshape(n_head, part, width), "head", split_axis=0, concat_axis=0, tiled=True)
    out_shape = jax.ShapeDtypeStruct((2, part, n_head * width), BF16)
    out = pl.pallas_call(
        lay_first_kernel,
        grid_spec=pltpu.PrefetchScalarGridSpec(
            num_scalar_prefetch=1,
            grid=(n_head,),
            in_specs=[pl.BlockSpec((part, width), lambda s, p: (0, 0))] * n_head,
            out_specs=pl.BlockSpec((1, part, width), lambda s, p: (0, 0, lax.rem(p[0] + n_head - s, n_head))),
        ),
        out_shape=out_shape,
        compiler_params=params,
        name="lay_first",
    )(place, *firsts)
    return pl.pallas_call(
        lay_second_kernel,
        grid=(1,),
        in_specs=[any_spec, pl.BlockSpec((n_head, part, width), lambda s: (0, 0, 0))],
        out_specs=any_spec,
        out_shape=out_shape,
        input_output_aliases={0: 0},
        scratch_shapes=[pltpu.SemaphoreType.DMA((n_head,))],
        compiler_params=params,
        name="lay_second",
    )(out, swapped)


def solution(mesh):
    heads = mesh.shape["head"]
    fine = Mesh(mesh.devices.reshape(heads, 4, 2, 4, 2), ("head", "z_hi", "z_lo", "y", "core"))
    tok = ("z_hi", "z_lo", "y", "core")
    placed = (
        P(None, tok, "head"),
        P(tok, "head"),
        P(tok, "head"),
        P("head", tok),
        P("head", None, None),
        P("head", None, None),
        P("head", None, None),
    )
    return jax.shard_map(
        local, mesh=fine, in_specs=placed, out_specs=P(None, tok + ("head",), None), check_vma=False
    )
```
